128 devices in a mesh: ep: 32 (over z, y, core), dp: 4 (over x).
Axes of the slice: x: 4, y: 4, z: 4, core: 2. Of those that a mesh axis runs over, the one named last changes fastest.
Arguments:
- tokens: bfloat16 [16384, 7168], P(('dp', 'ep')), parts along dimension 0, may hold values from -18 to 18
- expert_ids: int32 [16384, 2], P(('dp', 'ep')), parts along dimension 0, may hold values from 0 to 15, all different within a row; in each aligned block of 128 rows (0 to 127, 128 to 255, ...) at most 32 rows name the same one
- affinity: float32 [16384, 2], P(('dp', 'ep')), parts along dimension 0, may hold values from 0.05 to 1
- w_gate: bfloat16 [32, 7168, 512], P('ep'), may hold values from -0.0625 to 0.0625
- w_up: bfloat16 [32, 7168, 512], P('ep'), may hold values from -0.0625 to 0.0625
- w_down: bfloat16 [32, 512, 7168], P('ep'), may hold values from -0.1875 to 0.1875
Outputs:
- mixed: bfloat16 [16384, 7168], P(('dp', 'ep')), parts along dimension 0
The draws below stay inside these ranges and needn't reach their ends.
There are 4 independent parts, one for each index of `dp`. The reference program is written for one: setup_inputs(seed, part) draws one part's arguments, and reference() takes and returns one part's arrays. A program takes and returns all parts, laid end to end along the dimension named above; an argument that names none is the same for every part. Nothing has to cross between parts.
Inputs may be any that keep to these rules, and one draw needn't show every extreme that they name: `expert_ids`: each row names 2 different experts; among the rows of one index of ep no expert is named by more than 32 rows.
All inputs are finite; a program needn't handle non-finite values.
Results may differ from the reference program's by a relative error of at most 0.019.
Values may be sent and summed in bfloat16 or wider, within the bound.
No kernel may reach another device: no remote copies, remote signals or barrier semaphores. Data moves between devices by JAX's collectives and lax.ppermute only.
A program may use at most 256 MiB of HBM per device.

```python
import math
import jax
import jax.numpy as jnp
import numpy as np
from jax import lax

D = 7168
FF = 1024
TOP = 2
TOK_DEV = 128
FF_HALF = 512
EXPERTS = 16
CAP = 32
TOKENS = 4096
N_EP = 32


def draw_tokens(key, part):
    scale_key, block_key, value_key = jax.random.split(key, 3)
    row_scale = jnp.exp(jax.random.uniform(scale_key, (TOKENS, 1, 1), jnp.float32, jnp.log(0.8), jnp.log(1.25)))
    block_scale = jnp.exp(jax.random.uniform(block_key, (TOKENS, D // 16, 1), jnp.float32, jnp.log(0.05), jnp.log(2.0)))
    values = jnp.clip(jax.random.normal(value_key, (TOKENS, D // 16, 16), jnp.float32), -5.0, 5.0)
    return (values * block_scale * row_scale).reshape(TOKENS, D).astype(jnp.bfloat16)


def block_levels(own_key, shape, cuts, least, high):
    def one(dim, blocks):
        steps = jax.random.uniform(jax.random.fold_in(jax.random.fold_in(own_key, 6), dim), (blocks,), jnp.float32, least / len(cuts), high / len(cuts))
        return jnp.repeat(jnp.exp(steps), shape[dim] // blocks).reshape((-1,) + (1,) * (len(shape) - dim - 1))

    gain = one(*cuts[0])
    for cut in cuts[1:]:
        gain = gain * one(*cut)
    return gain


def deal_out(stream_key, own, number, rows, count, top, most, slope):
    ranking = jax.random.permutation(stream_key, count)
    crowded, usual = load_shares(count, rows * top, most, slope, True), load_shares(count, rows * top, most, slope, False)
    places = jnp.arange(count)

    def named(lengths, rotation):
        used = int((lengths > 0).sum())
        fixed = max(1, used // 4)
        passed = fixed + (places - fixed + rotation * (used - fixed)) % max(1, count - fixed)
        return jnp.zeros((count,), jnp.int32).at[ranking[jnp.where(places < fixed, places, passed)]].set(jnp.asarray(lengths, jnp.int32))

    lengths = jnp.where(number % 4 == 0, named(crowded, number // 4), named(usual, number - number // 4 - 1))
    mixed = jax.random.permutation(jax.random.fold_in(own, 3), count)
    donor, sink = mixed[0:count // 2 * 2:2], mixed[1:count // 2 * 2:2]
    room = jnp.minimum(lengths[donor] - 1, most - lengths[sink]) // 2
    room = jnp.where((donor == ranking[0]) | (sink == ranking[0]) | (lengths[sink] == 0), 0, jnp.maximum(room, 0))
    passed = jax.random.randint(jax.random.fold_in(own, 4), (count // 2,), 0, 1 << 20) % (room + 1)
    lengths = lengths.at[donor].add(-passed).at[sink].add(passed)
    labels = jnp.searchsorted(jnp.cumsum(lengths), jnp.arange(rows * top), side="right").astype(jnp.int32)
    grid = labels.reshape(top, rows).T
    grid = grid[jax.random.permutation(jax.random.fold_in(own, 1), rows)]
    rotation = jax.random.randint(jax.random.fold_in(own, 2), (rows, 1), 0, top)
    return jnp.take_along_axis(grid, (jnp.arange(top)[None, :] + rotation) % top, axis=1)


def load_shares(number_of, total, bound, lean, full):
    weights = [(1 << 20) // math.isqrt(standing ** lean) + 1 for standing in range(1, number_of + 1)]
    largest = bound if full else min(bound, max(-(-total // number_of), total * weights[0] // sum(weights)))
    least = 1 if total - largest >= number_of - 1 else 0
    counts, rest = [largest] + [least] * (number_of - 1), total - largest - least * (number_of - 1)
    while rest > 0:
        candidates = [i for i in range(1, number_of) if counts[i] < largest] or [i for i in range(1, number_of) if counts[i] < bound]
        mass, budget = sum([weights[i] for i in candidates]), rest
        for i in candidates:
            more = min(bound - counts[i], max(1, budget * weights[i] // mass), rest)
            counts[i] = counts[i] + more
            rest = rest - more
    return np.array(counts)


def noise(rng, extent, deviation, reach, cuts=(), kind=jnp.bfloat16):
    values = jax.random.normal(rng, extent, jnp.float32) * deviation
    if len(cuts) > 0:
        values = block_levels(rng, extent, cuts, -0.22, 0.18) * values
    return jnp.clip(values, min=-reach, max=reach).astype(kind)


def setup_inputs(seed: int = 0, part: int = 0) -> dict:
    streams_of = jax.random.split(jax.random.key(seed), 7)
    own_keys = jax.random.split(jax.random.fold_in(streams_of[6], part), 7)
    tokens = draw_tokens(jax.random.fold_in(jax.random.fold_in(streams_of[6], part), 71), part)
    expert_ids_keys = jax.random.split(jax.random.fold_in(own_keys[1], 1), TOKENS // TOK_DEV)
    expert_ids_turns = jax.random.permutation(jax.random.fold_in(own_keys[1], 3), TOKENS // TOK_DEV)
    expert_ids = jax.vmap(lambda own, number: deal_out(jax.random.fold_in(own_keys[1], 2), own, number, TOK_DEV, EXPERTS, TOP, CAP, 3))(expert_ids_keys, expert_ids_turns).reshape((TOKENS, TOP))
    affinity = jnp.clip(jnp.exp(math.log(1.0) - 2.9957323 * jax.random.uniform(own_keys[2], (TOKENS, TOP), jnp.float32) ** block_levels(own_keys[2], (TOKENS, TOP), ((0, 32),), -0.2, 0.2)), 0.05, 1.0)
    w_gate = noise(streams_of[3], (N_EP, D, FF_HALF), D ** -0.5, 0.0625, ((0, 32),))
    w_up = noise(streams_of[4], (N_EP, D, FF_HALF), D ** -0.5, 0.0625, ((0, 32),))
    w_down = noise(streams_of[5], (N_EP, FF_HALF, D), FF ** -0.5, 0.1875, ((0, 32),))
    return {"tokens": tokens, "expert_ids": expert_ids, "affinity": affinity, "w_gate": w_gate, "w_up": w_up, "w_down": w_down}


def quantize(tokens):
    count_rows = tokens.shape[0]
    blocks = tokens.astype(jnp.float32).reshape(count_rows, -1, 16)
    largest = jnp.max(jnp.abs(blocks), axis=2)
    scales = (jnp.maximum(largest, 0.25) / 9.0).astype(jnp.bfloat16)
    divided = blocks / scales.astype(jnp.float32)[:, :, None]
    payload = jnp.clip(divided, -6.0, 6.0).astype(jnp.bfloat16).reshape(count_rows, -1)
    return payload, scales


def restore(payload, scales):
    count_rows = payload.shape[0]
    values = payload.astype(jnp.float32).reshape(count_rows, -1, 16) * scales.astype(jnp.float32)[:, :, None]
    return values.astype(jnp.bfloat16).reshape(count_rows, -1)


def half_expert(restored, gate_half, up_half, down_half):
    gate = jnp.dot(restored, gate_half, preferred_element_type=jnp.float32)
    upward = jnp.dot(restored, up_half, preferred_element_type=jnp.float32)
    hidden = (jax.nn.silu(gate) * upward).astype(jnp.bfloat16)
    return jnp.dot(hidden, down_half, preferred_element_type=jnp.float32).astype(jnp.bfloat16)


def reference(tokens, expert_ids, affinity, w_gate, w_up, w_down):
    payload, scales = quantize(tokens)
    restored = restore(payload, scales)
    flat_ids = expert_ids.reshape(-1).astype(jnp.int32)
    assigned = flat_ids.shape[0]
    slot_total = N_EP * CAP

    def per_expert(expert):
        others = (flat_ids != expert).astype(jnp.int32)
        ordering = jnp.argsort(others, stable=True)[:slot_total].astype(jnp.int32)
        picked = restored[ordering // TOP]
        first_half = half_expert(picked, w_gate[2 * expert], w_up[2 * expert], w_down[2 * expert])
        second_half = half_expert(picked, w_gate[2 * expert + 1], w_up[2 * expert + 1], w_down[2 * expert + 1])
        summed = (first_half.astype(jnp.float32) + second_half.astype(jnp.float32)).astype(jnp.bfloat16)
        count_live = jnp.sum(1 - others)
        target_rows = jnp.where(jnp.arange(slot_total, dtype=jnp.int32) < count_live, ordering, assigned).astype(jnp.int32)
        return summed, target_rows

    outputs, targets = lax.map(per_expert, jnp.arange(EXPERTS, dtype=jnp.int32))
    per_slot = jnp.zeros((assigned, D), jnp.bfloat16).at[targets.reshape(-1)].set(outputs.reshape(-1, D), mode="drop")
    weights = affinity / jnp.sum(affinity, axis=1, keepdims=True)
    combined = jnp.sum(weights[:, :, None] * per_slot.astype(jnp.float32).reshape(TOKENS, TOP, D), axis=1)
    return combined.astype(jnp.bfloat16)
```

```python
import functools
import jax
import jax.numpy as jnp
from jax import lax
from jax.experimental import pallas as pl
from jax.experimental.pallas import tpu as pltpu
from jax.sharding import PartitionSpec as P

TOP = 2
BLOCK = 16
LANES = 128
VMEM_BYTES = 56 * 1024 * 1024


def iota(shape, dim):
    return lax.broadcasted_iota(jnp.int32, shape, dim)


def named(ids_ref, experts):
    ids = ids_ref[...]
    lanes = iota((ids.shape[0], experts), 1)
    hit = ids[:, 0:1] == lanes
    for k in range(1, TOP):
        hit = hit | (ids[:, k : k + 1] == lanes)
    return hit.astype(jnp.float32).astype(jnp.bfloat16)


def restored_lanes(values):
    x = values.astype(jnp.float32)
    lane = iota(x.shape, 1)
    top = jnp.abs(x)
    for bit in (1, 2, 4, 8):
        low = pltpu.roll(top, bit, 1)
        high = pltpu.roll(top, LANES - bit, 1)
        top = jnp.maximum(top, jnp.where((lane & bit) != 0, low, high))
    scale = (jnp.maximum(top, 0.25) / 9.0).astype(jnp.bfloat16).astype(jnp.float32)
    payload = jnp.clip(x / scale, -6.0, 6.0).astype(jnp.bfloat16).astype(jnp.float32)
    return (payload * scale).astype(jnp.bfloat16)


def send_kernel(experts, chunks, ids_ref, tokens_ref, *rest):
    out_refs, pick, restored = rest[:chunks], rest[chunks], rest[chunks + 1]
    count = tokens_ref.shape[0]
    rows = out_refs[0].shape[0]
    each = rows // experts

    @pl.when(pl.program_id(0) == 0)
    def _():
        mask = named(ids_ref, experts)
        before = (iota((count, count), 0) < iota((count, count), 1)).astype(jnp.float32)
        same = (iota((count, count), 0) == iota((count, count), 1)).astype(jnp.float32)
        dims = (((0,), (0,)), ((), ()))
        rank = lax.dot_general(
            mask, before.astype(jnp.bfloat16), dims, preferred_element_type=jnp.float32
        )
        turned = lax.dot_general(
            mask, same.astype(jnp.bfloat16), dims, preferred_element_type=jnp.float32
        )
        key = jnp.where(turned > 0.5, rank, -1.0).astype(jnp.bfloat16)
        spread = (iota((rows, experts), 0) // each == iota((rows, experts), 1)).astype(jnp.float32)
        wide = jnp.dot(spread.astype(jnp.bfloat16), key, preferred_element_type=jnp.float32)
        place = (iota((rows, count), 0) % each).astype(jnp.float32)
        for j in range(chunks):
            hit = (wide == place + float(each * j)).astype(jnp.float32)
            pick[j * rows : (j + 1) * rows, :] = hit.astype(jnp.bfloat16)

    for at in range(0, tokens_ref.shape[1], LANES):
        restored[:, at : at + LANES] = restored_lanes(tokens_ref[:, at : at + LANES])
    for j in range(chunks):
        out_refs[j][...] = jnp.dot(
            pick[j * rows : (j + 1) * rows, :],
            restored[...],
            preferred_element_type=jnp.float32,
        ).astype(jnp.bfloat16)


def slots_of_tokens(tokens, expert_ids, experts, slots, chunks):
    count, width = tokens.shape
    rows = experts * slots // chunks
    wide = 1024
    return pl.pallas_call(
        functools.partial(send_kernel, experts, chunks),
        name="send_slots",
        out_shape=[jax.ShapeDtypeStruct((rows, width), jnp.bfloat16)] * chunks,
        grid=(width // wide,),
        in_specs=[
            pl.BlockSpec((count, TOP), lambda d: (0, 0)),
            pl.BlockSpec((count, wide), lambda d: (0, d)),
        ],
        out_specs=[pl.BlockSpec((rows, wide), lambda d: (0, d))] * chunks,
        scratch_shapes=[
            pltpu.VMEM((rows * chunks, count), jnp.bfloat16),
            pltpu.VMEM((count, wide), jnp.bfloat16),
        ],
        compiler_params=pltpu.CompilerParams(
            dimension_semantics=("arbitrary",), vmem_limit_bytes=VMEM_BYTES
        ),
    )(expert_ids, tokens)


def expert_kernel(
    steps, x_ref, g0, g1, u0, u1, d0, d1, out_ref, gate0, gate1, up0, up1, hid0, hid1
):
    step = pl.program_id(0)
    pairs = ((gate0, g0), (gate1, g1), (up0, u0), (up1, u1))

    @pl.when(step == 0)
    def _():
        for total, _w in pairs:
            total[...] = jnp.zeros_like(total)

    @pl.when(step < steps)
    def _():
        x = x_ref[...]
        for total, w in pairs:
            total[...] += jnp.dot(x, w[...], preferred_element_type=jnp.float32)

    @pl.when(step == steps - 1)
    def _():
        for hid, gate, up in ((hid0, gate0, up0), (hid1, gate1, up1)):
            v = gate[...]
            hid[...] = (v / (1.0 + jnp.exp(-v)) * up[...]).astype(jnp.bfloat16)

    @pl.when(step >= steps)
    def _():
        out_ref[...] = (
            jnp.dot(hid0[...], d0[...], preferred_element_type=jnp.float32)
            + jnp.dot(hid1[...], d1[...], preferred_element_type=jnp.float32)
        ).astype(jnp.bfloat16)


def expert(rows, gates, ups, downs):
    count, width = rows.shape
    half = gates[0].shape[-1]
    wide = 1024
    steps = width // wide
    first = lambda s: jnp.minimum(s, steps - 1)
    second = lambda s: jnp.maximum(s - steps, 0)
    into = pl.BlockSpec((None, wide, half), lambda s: (0, first(s), 0))
    out_of = pl.BlockSpec((None, half, wide), lambda s: (0, 0, second(s)))
    return pl.pallas_call(
        functools.partial(expert_kernel, steps),
        name="expert_rows",
        out_shape=jax.ShapeDtypeStruct((count, width), jnp.bfloat16),
        grid=(2 * steps,),
        in_specs=[pl.BlockSpec((count, wide), lambda s: (0, first(s)))] + [into] * 4 + [out_of] * 2,
        out_specs=pl.BlockSpec((count, wide), lambda s: (0, second(s))),
        scratch_shapes=[pltpu.VMEM((count, half), jnp.float32)] * 4
        + [pltpu.VMEM((count, half), jnp.bfloat16)] * 2,
        compiler_params=pltpu.CompilerParams(
            dimension_semantics=("arbitrary",), vmem_limit_bytes=VMEM_BYTES
        ),
        cost_estimate=pl.CostEstimate(
            flops=count * width * half * 12,
            transcendentals=count * half * 2,
            bytes_accessed=width * half * 12 + count * width * 4,
        ),
    )(rows, *gates, *ups, *downs)


def mix_kernel(experts, chunks, ids_ref, affinity_ref, *rest):
    in_refs, out_ref, high, low = rest[:chunks], rest[chunks], rest[chunks + 1], rest[chunks + 2]
    count = out_ref.shape[0]
    rows = in_refs[0].shape[0]
    each = rows // experts

    @pl.when(pl.program_id(0) == 0)
    def _():
        mask = named(ids_ref, experts)
        after = (iota((count, count), 1) < iota((count, count), 0)).astype(jnp.float32)
        rank = jnp.dot(after.astype(jnp.bfloat16), mask, preferred_element_type=jnp.float32)
        key = jnp.where(mask.astype(jnp.float32) > 0.5, rank, -1.0).astype(jnp.bfloat16)
        affinity = affinity_ref[...]
        total = affinity[:, 0:1]
        for k in range(1, TOP):
            total = total + affinity[:, k : k + 1]
        lanes = iota((count, experts), 1)
        weight = jnp.zeros((count, experts), jnp.float32)
        for k in range(TOP):
            weight = jnp.where(
                ids_ref[:, k : k + 1] == lanes, affinity[:, k : k + 1] / total, weight
            )
        upper = weight.astype(jnp.bfloat16)
        lower = (weight - upper.astype(jnp.float32)).astype(jnp.bfloat16)
        spread = (iota((experts, rows), 1) // each == iota((experts, rows), 0)).astype(jnp.float32)
        spread = spread.astype(jnp.bfloat16)
        wide = jnp.dot(key, spread, preferred_element_type=jnp.float32)
        upper = jnp.dot(upper, spread, preferred_element_type=jnp.float32)
        lower = jnp.dot(lower, spread, preferred_element_type=jnp.float32)
        place = (iota((count, rows), 1) % each).astype(jnp.float32)
        for j in range(chunks):
            hit = wide == place + float(each * j)
            high[j] = jnp.where(hit, upper, 0.0).astype(jnp.bfloat16)
            low[j] = jnp.where(hit, lower, 0.0).astype(jnp.bfloat16)

    total = None
    for j in range(chunks):
        values = in_refs[j][...]
        part = jnp.dot(high[j], values, preferred_element_type=jnp.float32) + jnp.dot(
            low[j], values, preferred_element_type=jnp.float32
        )
        total = part if total is None else total + part
    out_ref[...] = total.astype(jnp.bfloat16)


def mix(expert_ids, affinity, parts, experts):
    count = expert_ids.shape[0]
    rows, width = parts[0].shape
    chunks = len(parts)
    wide = 1024
    return pl.pallas_call(
        functools.partial(mix_kernel, experts, chunks),
        name="mix_slots",
        out_shape=jax.ShapeDtypeStruct((count, width), jnp.bfloat16),
        grid=(width // wide,),
        in_specs=[pl.BlockSpec((count, TOP), lambda d: (0, 0))] * 2
        + [pl.BlockSpec((rows, wide), lambda d: (0, d))] * chunks,
        out_specs=pl.BlockSpec((count, wide), lambda d: (0, d)),
        scratch_shapes=[pltpu.VMEM((chunks, count, rows), jnp.bfloat16)] * 2,
        compiler_params=pltpu.CompilerParams(
            dimension_semantics=("arbitrary",), vmem_limit_bytes=VMEM_BYTES
        ),
    )(expert_ids, affinity, *parts)


def exchange(rows, devices):
    count, width = rows.shape
    split = rows.reshape(devices, count // devices, width)
    return lax.all_to_all(split, "ep", split_axis=0, concat_axis=0, tiled=True).reshape(
        count, width
    )


CHUNKS = 2


def on_device(tokens, expert_ids, affinity, w_gate, w_up, w_down):
    devices = lax.axis_size("ep")
    experts = devices // 2
    slots = 2 * tokens.shape[0] * TOP // experts
    pairs = [(s, s ^ 1) for s in range(devices)]
    gates, ups, downs = [(w, lax.ppermute(w, "ep", pairs)) for w in (w_gate, w_up, w_down)]
    sent = slots_of_tokens(tokens, expert_ids, experts, slots, CHUNKS)
    parts = []
    for rows in sent:
        computed = expert(exchange(rows, devices), gates, ups, downs)
        parts.append(exchange(computed, devices))
    return mix(expert_ids, affinity, parts, experts)


def solution(mesh):
    rows = P(("dp", "ep"), None)
    weights = P("ep", None, None)
    return jax.shard_map(
        on_device,
        mesh=mesh,
        in_specs=(rows, rows, rows, weights, weights, weights),
        out_specs=rows,
        check_vma=False,
    )
```

```python
import functools
import jax
import jax.numpy as jnp
from jax import lax
from jax.experimental import pallas as pl
from jax.experimental.pallas import tpu as pltpu
from jax.sharding import PartitionSpec as P

TOP = 2
BLOCK = 16
LANES = 128
VMEM_BYTES = 56 * 1024 * 1024


def iota(shape, dim):
    return lax.broadcasted_iota(jnp.int32, shape, dim)


def halves(value):
    upper = value.astype(jnp.bfloat16)
    return upper, (value - upper.astype(jnp.float32)).astype(jnp.bfloat16)


def ones_where(hit):
    return hit.astype(jnp.float32).astype(jnp.bfloat16)


def times(a, b):
    return jnp.dot(a, b, preferred_element_type=jnp.float32)


def slot_keys(turned_ids_ref, experts):
    count = turned_ids_ref.shape[1]
    row = iota((experts, count), 0)
    hit = turned_ids_ref[0:1, :] == row
    for k in range(1, TOP):
        hit = hit | (turned_ids_ref[k : k + 1, :] == row)
    earlier = ones_where(iota((count, count), 0) < iota((count, count), 1))
    rank = times(ones_where(hit), earlier)
    return jnp.where(hit, rank, -1.0).astype(jnp.bfloat16)


def restored_rows(tokens, gather, spread, spread3):
    x = tokens.astype(jnp.float32)
    width = x.shape[1]
    tops = []
    for at in range(0, width, LANES):
        top = jnp.abs(x[:, at : at + LANES])
        for step in (1, 2, 4, 8):
            top = jnp.maximum(top, pltpu.roll(top, LANES - step, 1))
        tops.append(top.astype(jnp.bfloat16))
    largest = times(jnp.concatenate(tops, axis=1), gather)
    scale = (jnp.maximum(largest, 0.25) / 9.0).astype(jnp.bfloat16)
    inverse = 1.0 / scale.astype(jnp.float32)
    first, rest = halves(inverse)
    second, third = halves(inverse - first.astype(jnp.float32))
    inverse = times(jnp.concatenate([first, second, third], axis=1), spread3)
    scale = times(scale, spread)
    payload = jnp.clip(x * inverse, -6.0, 6.0).astype(jnp.bfloat16).astype(jnp.float32)
    return (payload * scale).astype(jnp.bfloat16)


def send_kernel(experts, chunks, ids_ref, tokens_ref, *rest):
    out_refs, (pick, gather, spread, spread3) = rest[:chunks], rest[chunks:]
    count, width = tokens_ref.shape
    rows = out_refs[0].shape[0]
    each = rows // experts
    blocks = width // BLOCK

    @pl.when(pl.program_id(0) == 0)
    def _():
        key = slot_keys(ids_ref, experts)
        wide = times(ones_where(iota((rows, experts), 0) // each == iota((rows, experts), 1)), key)
        place = (iota((rows, count), 0) % each).astype(jnp.float32)
        for j in range(chunks):
            pick[j * rows : (j + 1) * rows, :] = ones_where(wide == place + float(each * j))
        gather[...] = ones_where(iota((width, blocks), 0) == BLOCK * iota((width, blocks), 1))
        spread[...] = ones_where(iota((blocks, width), 1) // BLOCK == iota((blocks, width), 0))
        for j in range(3):
            spread3[j * blocks : (j + 1) * blocks, :] = spread[...]

    restored = restored_rows(tokens_ref[...], gather[...], spread[...], spread3[...])
    for j in range(chunks):
        out_refs[j][...] = times(pick[j * rows : (j + 1) * rows, :], restored).astype(jnp.bfloat16)


def slots_of_tokens(tokens, turned_ids, experts, slots, chunks):
    count, width = tokens.shape
    rows = experts * slots // chunks
    wide = 1024
    blocks = wide // BLOCK
    return pl.pallas_call(
        functools.partial(send_kernel, experts, chunks),
        name="send_slots",
        out_shape=[jax.ShapeDtypeStruct((rows, width), jnp.bfloat16)] * chunks,
        grid=(width // wide,),
        in_specs=[
            pl.BlockSpec((TOP, count), lambda d: (0, 0)),
            pl.BlockSpec((count, wide), lambda d: (0, d)),
        ],
        out_specs=[pl.BlockSpec((rows, wide), lambda d: (0, d))] * chunks,
        scratch_shapes=[
            pltpu.VMEM((rows * chunks, count), jnp.bfloat16),
            pltpu.VMEM((wide, blocks), jnp.bfloat16),
            pltpu.VMEM((blocks, wide), jnp.bfloat16),
            pltpu.VMEM((3 * blocks, wide), jnp.bfloat16),
        ],
        compiler_params=pltpu.CompilerParams(
            dimension_semantics=("arbitrary",), vmem_limit_bytes=VMEM_BYTES
        ),
    )(turned_ids, tokens)


def expert_kernel(
    steps, x_ref, g0, g1, u0, u1, d0, d1, out_ref, gate0, gate1, up0, up1, hid0, hid1
):
    step = pl.program_id(0)
    pairs = ((gate0, g0), (gate1, g1), (up0, u0), (up1, u1))

    @pl.when(step == 0)
    def _():
        for total, _w in pairs:
            total[...] = jnp.zeros_like(total)

    @pl.when(step < steps)
    def _():
        x = x_ref[...]
        for total, w in pairs:
            total[...] += jnp.dot(x, w[...], preferred_element_type=jnp.float32)

    @pl.when(step == steps - 1)
    def _():
        for hid, gate, up in ((hid0, gate0, up0), (hid1, gate1, up1)):
            v = gate[...]
            hid[...] = (v / (1.0 + jnp.exp(-v)) * up[...]).astype(jnp.bfloat16)

    @pl.when(step >= steps)
    def _():
        out_ref[...] = (
            jnp.dot(hid0[...], d0[...], preferred_element_type=jnp.float32)
            + jnp.dot(hid1[...], d1[...], preferred_element_type=jnp.float32)
        ).astype(jnp.bfloat16)


def expert(rows, gates, ups, downs):
    count, width = rows.shape
    half = gates[0].shape[-1]
    wide = 1024
    steps = width // wide
    first = lambda s: jnp.minimum(s, steps - 1)
    second = lambda s: jnp.maximum(s - steps, 0)
    into = pl.BlockSpec((None, wide, half), lambda s: (0, first(s), 0))
    out_of = pl.BlockSpec((None, half, wide), lambda s: (0, 0, second(s)))
    return pl.pallas_call(
        functools.partial(expert_kernel, steps),
        name="expert_rows",
        out_shape=jax.ShapeDtypeStruct((count, width), jnp.bfloat16),
        grid=(2 * steps,),
        in_specs=[pl.BlockSpec((count, wide), lambda s: (0, first(s)))] + [into] * 4 + [out_of] * 2,
        out_specs=pl.BlockSpec((count, wide), lambda s: (0, second(s))),
        scratch_shapes=[pltpu.VMEM((count, half), jnp.float32)] * 4
        + [pltpu.VMEM((count, half), jnp.bfloat16)] * 2,
        compiler_params=pltpu.CompilerParams(
            dimension_semantics=("arbitrary",), vmem_limit_bytes=VMEM_BYTES
        ),
        cost_estimate=pl.CostEstimate(
            flops=count * width * half * 12,
            transcendentals=count * half * 2,
            bytes_accessed=width * half * 12 + count * width * 4,
        ),
    )(rows, *gates, *ups, *downs)


def table_kernel(experts, chunks, ids_ref, affinity_ref, out_ref):
    count = ids_ref.shape[1]
    rows = out_ref.shape[2]
    each = rows // experts
    key = slot_keys(ids_ref, experts)
    total = affinity_ref[0:1, :]
    for k in range(1, TOP):
        total = total + affinity_ref[k : k + 1, :]
    row = iota((experts, count), 0)
    weight = jnp.zeros((experts, count), jnp.float32)
    for k in range(TOP):
        share = affinity_ref[k : k + 1, :] / total
        weight = jnp.where(ids_ref[k : k + 1, :] == row, share, weight)
    same = ones_where(iota((count, count), 0) == iota((count, count), 1))
    spread = ones_where(iota((experts, rows), 1) // each == iota((experts, rows), 0))

    def by_token(value):
        turned = lax.dot_general(
            same, value, (((1,), (1,)), ((), ())), preferred_element_type=jnp.float32
        )
        return times(turned.astype(jnp.bfloat16), spread)

    wide = by_token(key)
    upper, lower = [by_token(part) for part in halves(weight)]
    place = (iota((count, rows), 1) % each).astype(jnp.float32)
    for j in range(chunks):
        hit = wide == place + float(each * j)
        out_ref[j, 0:count, :] = jnp.where(hit, upper, 0.0).astype(jnp.bfloat16)
        out_ref[j, count : 2 * count, :] = jnp.where(hit, lower, 0.0).astype(jnp.bfloat16)


def weights_of_slots(turned_ids, turned_affinity, experts, slots, chunks):
    count = turned_ids.shape[1]
    rows = experts * slots // chunks
    return pl.pallas_call(
        functools.partial(table_kernel, experts, chunks),
        name="slot_weights",
        out_shape=jax.ShapeDtypeStruct((chunks, 2 * count, rows), jnp.bfloat16),
    )(turned_ids, turned_affinity)


def mix_kernel(chunks, table_ref, *rest):
    in_refs, out_ref = rest[:chunks], rest[chunks]
    count = out_ref.shape[0]
    total = times(table_ref[0], in_refs[0][...])
    for j in range(1, chunks):
        total = total + times(table_ref[j], in_refs[j][...])
    out_ref[...] = (total[:count] + total[count:]).astype(jnp.bfloat16)


def mix(table, parts):
    chunks, count, rows = table.shape
    count //= 2
    width = parts[0].shape[1]
    wide = 1024
    return pl.pallas_call(
        functools.partial(mix_kernel, chunks),
        name="mix_slots",
        out_shape=jax.ShapeDtypeStruct((count, width), jnp.bfloat16),
        grid=(width // wide,),
        in_specs=[pl.BlockSpec(table.shape, lambda d: (0, 0, 0))]
        + [pl.BlockSpec((rows, wide), lambda d: (0, d))] * chunks,
        out_specs=pl.BlockSpec((count, wide), lambda d: (0, d)),
        compiler_params=pltpu.CompilerParams(
            dimension_semantics=("arbitrary",), vmem_limit_bytes=VMEM_BYTES
        ),
    )(table, *parts)


def exchange(rows, devices):
    count, width = rows.shape
    split = rows.reshape(devices, count // devices, width)
    return lax.all_to_all(split, "ep", split_axis=0, concat_axis=0, tiled=True).reshape(
        count, width
    )


CHUNKS = 2


def on_device(tokens, expert_ids, affinity, w_gate, w_up, w_down):
    devices = lax.axis_size("ep")
    experts = devices // 2
    slots = 2 * tokens.shape[0] * TOP // experts
    pairs = [(s, s ^ 1) for s in range(devices)]
    gates, ups, downs = [(w, lax.ppermute(w, "ep", pairs)) for w in (w_gate, w_up, w_down)]
    turned_ids = expert_ids.T
    table = weights_of_slots(turned_ids, affinity.T, experts, slots, CHUNKS)
    sent = slots_of_tokens(tokens, turned_ids, experts, slots, CHUNKS)
    parts = []
    for rows in sent:
        computed = expert(exchange(rows, devices), gates, ups, downs)
        parts.append(exchange(computed, devices))
    return mix(table, parts)


def solution(mesh):
    rows = P(("dp", "ep"), None)
    weights = P("ep", None, None)
    return jax.shard_map(
        on_device,
        mesh=mesh,
        in_specs=(rows, rows, rows, weights, weights, weights),
        out_specs=rows,
        check_vma=False,
    )
```

```python
import functools
import math
import jax
import jax.numpy as jnp
import numpy as np
from jax import lax
from jax.experimental import pallas as pl
from jax.experimental.pallas import tpu as pltpu
from jax.sharding import PartitionSpec as P

TOP = 2
BLOCK = 16
LANES = 128
CHUNKS = 2
VMEM_BYTES = 56 * 1024 * 1024
OFFSETS = (0, 1, -1, 2)
PARAMS = pltpu.CompilerParams(
    dimension_semantics=("arbitrary",), vmem_limit_bytes=VMEM_BYTES
)


def iota(shape, dim):
    return lax.broadcasted_iota(jnp.int32, shape, dim)


def halves(value):
    upper = value.astype(jnp.bfloat16)
    return upper, (value - upper.astype(jnp.float32)).astype(jnp.bfloat16)


def ones_where(hit):
    return hit.astype(jnp.float32).astype(jnp.bfloat16)


def times(a, b):
    return jnp.dot(a, b, preferred_element_type=jnp.float32)


def times_turned(a, b):
    return lax.dot_general(a, b, (((1,), (1,)), ((), ())), preferred_element_type=jnp.float32)


def restored_rows(tokens, gather, spread, spread3):
    x = tokens.astype(jnp.float32)
    tops = []
    for at in range(0, x.shape[1], LANES):
        top = jnp.abs(x[:, at : at + LANES])
        for step in (1, 2, 4, 8):
            top = jnp.maximum(top, pltpu.roll(top, LANES - step, 1))
        tops.append(top.astype(jnp.bfloat16))
    largest = times(jnp.concatenate(tops, axis=1), gather)
    scale = (jnp.maximum(largest, 0.25) / 9.0).astype(jnp.bfloat16)
    inverse = 1.0 / scale.astype(jnp.float32)
    first, rest = halves(inverse)
    second, third = halves(inverse - first.astype(jnp.float32))
    inverse = times(jnp.concatenate([first, second, third], axis=1), spread3)
    scale = times(scale, spread)
    payload = jnp.clip(x * inverse, -6.0, 6.0).astype(jnp.bfloat16).astype(jnp.float32)
    return (payload * scale).astype(jnp.bfloat16)


def restore_kernel(wide, ids_ref, affinity_ref, tokens_ref, a_ref, b_ref):
    count, half = tokens_ref.shape
    blocks = wide // BLOCK
    gather = ones_where(iota((wide, blocks), 0) == BLOCK * iota((wide, blocks), 1))
    spread = ones_where(iota((blocks, wide), 1) // BLOCK == iota((blocks, wide), 0))
    spread3 = jnp.concatenate([spread] * 3, axis=0)

    def fill(out_ref):
        for at in range(0, half, wide):
            out_ref[:, at : at + wide] = restored_rows(
                tokens_ref[:, at : at + wide], gather, spread, spread3
            )
        ids = ids_ref[...].astype(jnp.float32)
        affinity = affinity_ref[...]
        total = affinity[0:1, :]
        for k in range(1, TOP):
            total = total + affinity[k : k + 1, :]
        lines = [ids[k : k + 1, :].astype(jnp.bfloat16) for k in range(TOP)]
        for k in range(TOP):
            lines.extend(halves(affinity[k : k + 1, :] / total))
        row = iota((BLOCK, count), 0)
        turned = jnp.zeros((BLOCK, count), jnp.float32)
        for j, line in enumerate(lines):
            turned = jnp.where(row == j, line.astype(jnp.float32), turned)
        same = ones_where(iota((count, count), 0) == iota((count, count), 1))
        by_token = times_turned(same, turned.astype(jnp.bfloat16)).astype(jnp.bfloat16)
        place = ones_where(iota((BLOCK, LANES), 0) == iota((BLOCK, LANES), 1))
        out_ref[:, half : half + LANES] = times(by_token, place).astype(jnp.bfloat16)

    @pl.when(pl.program_id(0) == 0)
    def _():
        fill(a_ref)

    @pl.when(pl.program_id(0) == 1)
    def _():
        fill(b_ref)


def restore(tokens, turned_ids, turned_affinity):
    count, width = tokens.shape
    half = width // 2
    wide = half // 4
    small = pl.BlockSpec((TOP, count), lambda h: (0, 0))
    out = jax.ShapeDtypeStruct((count, half + LANES), jnp.bfloat16)
    return pl.pallas_call(
        functools.partial(restore_kernel, wide),
        name="restore_tokens",
        out_shape=[out, out],
        grid=(2,),
        in_specs=[small, small, pl.BlockSpec((count, half), lambda h: (0, h))],
        out_specs=[pl.BlockSpec((count, half + LANES), lambda h: (0, 0))] * 2,
        compiler_params=PARAMS,
    )(turned_ids, turned_affinity, tokens)


def slot_tables(meta, targets, side):
    count = meta.shape[0]
    each = count * TOP * 2 // (side * side) // CHUNKS
    rows = side * each
    pickers = ones_where(iota((BLOCK, LANES), 0) == iota((BLOCK, LANES), 1))
    lines = times_turned(pickers, meta)
    hit = None
    upper = lower = jnp.zeros((side, count), jnp.float32)
    for k in range(TOP):
        this = lines[k : k + 1, :] == targets
        upper = jnp.where(this, lines[TOP + 2 * k : TOP + 2 * k + 1, :], upper)
        lower = jnp.where(this, lines[TOP + 2 * k + 1 : TOP + 2 * k + 2, :], lower)
        hit = this if hit is None else hit | this
    earlier = ones_where(iota((count, count), 0) < iota((count, count), 1))
    rank = times(ones_where(hit), earlier)
    key = jnp.where(hit, rank, -1.0).astype(jnp.bfloat16)
    row = iota((CHUNKS * rows, side), 0)
    spread = ones_where((row % rows) // each == iota((CHUNKS * rows, side), 1))
    place = iota((CHUNKS * rows, count), 0)
    place = ((place // rows) * each + place % each).astype(jnp.float32)
    hits = times(spread, key) == place
    return hits, times(spread, upper.astype(jnp.bfloat16)), times(spread, lower.astype(jnp.bfloat16))


def pick_kernel(side, targets_ref, *rest):
    ins, outs, picks = rest[:18], rest[18:-1], rest[-1]
    step = pl.program_id(0)
    rows = picks.shape[2] // CHUNKS
    each = rows // side

    @pl.when(step == 0)
    def _():
        for h in range(2):
            own = ins[9 * h : 9 * h + 9]
            notes = (own[3], own[4], own[5], own[8])
            targets = targets_ref[side * h : side * h + side, :]
            for i, note in enumerate(notes):
                hits, _u, _l = slot_tables(note[...], targets, side)
                picks[h, i] = ones_where(hits)

    for h in range(2):
        own = ins[9 * h : 9 * h + 9]
        opposite = jnp.where(step < 2, own[6][...], own[7][...])
        for i, block in enumerate((own[0][...], own[1][...], own[2][...], opposite)):
            found = times(picks[h, i], block).astype(jnp.bfloat16)
            for j in range(CHUNKS):
                for o in range(side):
                    at = j * rows + o * each
                    outs[(j * 2 + h) * side + o][i * each : (i + 1) * each, :] = found[
                        at : at + each
                    ]


def pick_slots(targets, gathered, side):
    count, padded = gathered[0][0].shape
    half = padded - LANES
    wide = half // 4
    each = count * TOP * 2 // (side * side) // CHUNKS
    rows = side * each
    note = pl.BlockSpec((count, LANES), lambda q: (0, half // LANES))
    late_note = pl.BlockSpec((count, LANES), lambda q: (0, half // 2 // LANES))
    data = pl.BlockSpec((count, wide), lambda q: (0, q))
    first = pl.BlockSpec((count, wide), lambda q: (0, jnp.minimum(q, 1)))
    second = pl.BlockSpec((count, wide), lambda q: (0, jnp.maximum(q - 2, 0)))
    specs, args = [pl.BlockSpec(targets.shape, lambda q: (0, 0))], [targets]
    for own, back, ahead, piece1, piece2 in gathered:
        specs += [data] * 3 + [note] * 3 + [first, second, late_note]
        args += [own, back, ahead, own, back, ahead, piece1, piece2, piece2]
    outs = pl.pallas_call(
        functools.partial(pick_kernel, side),
        name="pick_slots",
        out_shape=[jax.ShapeDtypeStruct((rows, half), jnp.bfloat16)] * (CHUNKS * 2 * side),
        grid=(4,),
        in_specs=specs,
        out_specs=[pl.BlockSpec((rows, wide), lambda q: (0, q))] * (CHUNKS * 2 * side),
        scratch_shapes=[pltpu.VMEM((2, side, CHUNKS * rows, count), jnp.bfloat16)],
        compiler_params=PARAMS,
    )(*args)
    return [
        [[outs[(j * 2 + h) * side + o] for o in range(side)] for h in range(2)]
        for j in range(CHUNKS)
    ]


def expert_kernel(side, steps, *refs):
    a_in, b_in = refs[:side], refs[side : 2 * side]
    g0, g1, u0, u1, d0, d1 = refs[2 * side : 2 * side + 6]
    a_out, b_out = refs[2 * side + 6 : 3 * side + 6], refs[3 * side + 6 : 4 * side + 6]
    x, gate0, gate1, up0, up1, hid0, hid1 = refs[4 * side + 6 :]
    step = pl.program_id(0)
    rows = a_in[0].shape[0]
    each = rows // side
    pairs = ((gate0, g0), (gate1, g1), (up0, u0), (up1, u1))

    @pl.when(step == 0)
    def _():
        for total, _w in pairs:
            total[...] = jnp.zeros_like(total)

    @pl.when(step < steps // 2)
    def _():
        for p in range(side):
            x[p * rows : (p + 1) * rows, :] = a_in[p][...]

    @pl.when((step >= steps // 2) & (step < steps))
    def _():
        for p in range(side):
            for q in range(side):
                at = p * rows + q * each
                x[at : at + each, :] = b_in[q][p * each : (p + 1) * each, :]

    @pl.when(step < steps)
    def _():
        for total, w in pairs:
            total[...] += times(x[...], w[...])

    @pl.when(step == steps - 1)
    def _():
        for hid, gate, up in ((hid0, gate0, up0), (hid1, gate1, up1)):
            v = gate[...]
            hid[...] = (v / (1.0 + jnp.exp(-v)) * up[...]).astype(jnp.bfloat16)

    def down():
        return (times(hid0[...], d0[...]) + times(hid1[...], d1[...])).astype(jnp.bfloat16)

    @pl.when((step >= steps) & (step < steps + steps // 2))
    def _():
        y = down()
        for p in range(side):
            a_out[p][...] = y[p * rows : (p + 1) * rows]

    @pl.when(step >= steps + steps // 2)
    def _():
        y = down()
        for p in range(side):
            for q in range(side):
                at = p * rows + q * each
                b_out[q][p * each : (p + 1) * each, :] = y[at : at + each]


def expert(parts, gates, ups, downs):
    a_rows, b_rows = parts
    side = len(a_rows)
    rows, half = a_rows[0].shape
    hidden = gates.shape[-1]
    count = side * rows
    wide = half // 4
    steps = 2 * half // wide
    clamp = lambda s, start: jnp.clip(s - start, 0, steps // 2 - 1)
    block = lambda start: pl.BlockSpec((rows, wide), lambda s: (0, clamp(s, start)))
    into = [
        pl.BlockSpec((None, wide, hidden), lambda s, c=c: (c, jnp.minimum(s, steps - 1), 0))
        for c in range(2)
    ]
    out_of = [
        pl.BlockSpec((None, hidden, wide), lambda s, c=c: (c, 0, jnp.maximum(s - steps, 0)))
        for c in range(2)
    ]
    outs = pl.pallas_call(
        functools.partial(expert_kernel, side, steps),
        name="expert_rows",
        out_shape=[jax.ShapeDtypeStruct((rows, half), jnp.bfloat16)] * (2 * side),
        grid=(2 * steps,),
        in_specs=[block(0)] * side + [block(steps // 2)] * side + into * 2 + out_of,
        out_specs=[block(steps)] * side + [block(steps + steps // 2)] * side,
        scratch_shapes=[pltpu.VMEM((count, wide), jnp.bfloat16)]
        + [pltpu.VMEM((count, hidden), jnp.float32)] * 4
        + [pltpu.VMEM((count, hidden), jnp.bfloat16)] * 2,
        compiler_params=PARAMS,
        cost_estimate=pl.CostEstimate(
            flops=count * half * hidden * 24,
            transcendentals=count * hidden * 2,
            bytes_accessed=half * hidden * 24 + count * half * 8,
        ),
    )(*a_rows, *b_rows, gates, gates, ups, ups, downs, downs)
    return outs[:side], outs[side:]


def weight_kernel(side, targets_ref, *rest):
    notes, out_ref = rest[:-1], rest[-1]
    count = notes[0].shape[0]
    same = ones_where(iota((count, count), 0) == iota((count, count), 1))
    for h in range(2):
        targets = targets_ref[side * h : side * h + side, :]
        for i in range(side):
            hits, upper, lower = slot_tables(notes[h * side + i][...], targets, side)
            for j, part in enumerate((upper, lower)):
                turned = times_turned(same, jnp.where(hits, part, 0.0).astype(jnp.bfloat16))
                out_ref[h, i, j * count : (j + 1) * count, :] = turned.astype(jnp.bfloat16)


def weights_of_slots(targets, gathered, side):
    count, padded = gathered[0][0].shape
    half = padded - LANES
    slots = side * count * TOP * 2 // (side * side)
    note = pl.BlockSpec((count, LANES), lambda q: (0, half // LANES))
    late_note = pl.BlockSpec((count, LANES), lambda q: (0, half // 2 // LANES))
    args = [targets]
    for own, back, ahead, piece1, piece2 in gathered:
        args += [own, back, ahead, piece2]
    shape = (2, side, 2 * count, slots)
    return pl.pallas_call(
        functools.partial(weight_kernel, side),
        name="slot_weights",
        out_shape=jax.ShapeDtypeStruct(shape, jnp.bfloat16),
        grid=(1,),
        in_specs=[pl.BlockSpec(targets.shape, lambda q: (0, 0))]
        + ([note] * 3 + [late_note]) * 2,
        out_specs=pl.BlockSpec(shape, lambda q: (0, 0, 0, 0)),
        compiler_params=PARAMS,
    )(*args)


def partial_kernel(side, table_ref, *rest):
    ins = rest[: CHUNKS * 2 * side]
    outs = rest[CHUNKS * 2 * side :]
    count = table_ref.shape[2] // 2
    rows = ins[0].shape[0]
    each = rows // side
    step = pl.program_id(0)
    for h in range(2):
        own, back, ahead, piece1, piece2 = outs[5 * h : 5 * h + 5]
        for i in range(side):
            values = jnp.concatenate(
                [
                    ins[(j * 2 + h) * side + o][i * each : (i + 1) * each, :]
                    for j in range(CHUNKS)
                    for o in range(side)
                ],
                axis=0,
            )
            both = times(table_ref[h, i], values)
            total = both[:count] + both[count:]
            if i == 0:
                own[...] = total
            elif i < 3:
                (back, ahead)[i - 1][...] = total.astype(jnp.bfloat16)
            else:
                pl.when(step < 2)(
                    lambda r=piece1, t=total: r.__setitem__(Ellipsis, t.astype(jnp.bfloat16))
                )
                pl.when(step >= 2)(
                    lambda r=piece2, t=total: r.__setitem__(Ellipsis, t.astype(jnp.bfloat16))
                )


def partial_sums(table, parts):
    side = table.shape[1]
    count = table.shape[2] // 2
    rows, half = parts[0][0][0].shape
    wide = half // 4
    data = pl.BlockSpec((rows, wide), lambda q: (0, q))
    whole = pl.BlockSpec((count, wide), lambda q: (0, q))
    first = pl.BlockSpec((count, wide), lambda q: (0, jnp.minimum(q, 1)))
    second = pl.BlockSpec((count, wide), lambda q: (0, jnp.maximum(q - 2, 0)))
    shape = lambda w, t: jax.ShapeDtypeStruct((count, w), t)
    bf16 = jnp.bfloat16
    outs = pl.pallas_call(
        functools.partial(partial_kernel, side),
        name="partial_sums",
        out_shape=[
            shape(half, jnp.float32),
            shape(half, bf16),
            shape(half, bf16),
            shape(half // 2, bf16),
            shape(half // 2, bf16),
        ]
        * 2,
        grid=(4,),
        in_specs=[pl.BlockSpec(table.shape, lambda q: (0, 0, 0, 0))]
        + [data] * (CHUNKS * 2 * side),
        out_specs=[whole, whole, whole, first, second] * 2,
        compiler_params=PARAMS,
    )(table, *[p for chunk in parts for ring in chunk for p in ring])
    return outs[:5], outs[5:]


def add_kernel(*refs):
    step = pl.program_id(0)
    for h in range(2):
        back, ahead, piece1, piece2 = refs[4 * h : 4 * h + 4]
        back_out, ahead_out = refs[8 + 2 * h : 10 + 2 * h]

        def joined(base, piece):
            return (base[...].astype(jnp.float32) + piece[...].astype(jnp.float32)).astype(
                jnp.bfloat16
            )

        @pl.when(step == 0)
        def _():
            ahead_out[...] = joined(ahead, piece1)
            back_out[...] = back[...]

        @pl.when(step == 1)
        def _():
            back_out[...] = joined(back, piece2)
            ahead_out[...] = ahead[...]


def add_pieces(groups):
    count, half = groups[0][0].shape
    data = pl.BlockSpec((count, half // 2), lambda q: (0, q))
    piece = pl.BlockSpec((count, half // 2), lambda q: (0, 0))
    outs = pl.pallas_call(
        add_kernel,
        name="add_pieces",
        out_shape=[jax.ShapeDtypeStruct((count, half), jnp.bfloat16)] * 4,
        grid=(2,),
        in_specs=[data, data, piece, piece] * 2,
        out_specs=[data] * 4,
        compiler_params=PARAMS,
    )(*groups[0], *groups[1])
    return outs[:2], outs[2:]


def sum_kernel(steps, *refs):
    out_ref = refs[-1]
    step = pl.program_id(0)
    for h in range(2):

        @pl.when(step // steps == h)
        def _():
            own, one, two = refs[3 * h : 3 * h + 3]
            out_ref[...] = (
                own[...] + one[...].astype(jnp.float32) + two[...].astype(jnp.float32)
            ).astype(jnp.bfloat16)


def final_sum(groups):
    count, half = groups[0][0].shape
    steps = 2
    wide = half // steps
    first = pl.BlockSpec((count, wide), lambda q: (0, jnp.minimum(q, steps - 1)))
    second = pl.BlockSpec((count, wide), lambda q: (0, jnp.maximum(q - steps, 0)))
    return pl.pallas_call(
        functools.partial(sum_kernel, steps),
        name="final_sum",
        out_shape=jax.ShapeDtypeStruct((count, 2 * half), jnp.bfloat16),
        grid=(2 * steps,),
        in_specs=[first] * 3 + [second] * 3,
        out_specs=pl.BlockSpec((count, wide), lambda q: (0, q)),
        compiler_params=PARAMS,
    )(*groups[0], *groups[1])


def on_device(tokens, expert_ids, affinity, w_gate, w_up, w_down):
    devices = lax.axis_size("ep")
    side = math.isqrt(devices // 2)
    half = tokens.shape[1] // 2

    def move(value, ring, offset):
        pairs = []
        for s in range(devices):
            z, y, core = s // 2 // side, s // 2 % side, s % 2
            z, y = ((z, (y + offset) % side), ((z + offset) % side, y))[ring]
            pairs.append((s, (z * side + y) * 2 + core))
        return lax.ppermute(value, "ep", pairs)

    experts = np.zeros((devices, 2 * side), np.float32)
    for s in range(devices):
        z, y = s // 2 // side, s // 2 % side
        experts[s, :side] = [(z + o) % side * side + y for o in OFFSETS]
        experts[s, side:] = [z * side + (y + o) % side for o in OFFSETS]
    targets = jnp.asarray(experts)[lax.axis_index("ep")]
    targets = jnp.broadcast_to(targets[:, None], (2 * side, tokens.shape[0]))

    mates = [[s, s + 1] for s in range(0, devices, 2)]
    gates, ups, downs = [
        lax.all_gather(w, "ep", axis_index_groups=mates, axis=0, tiled=True)
        for w in (w_gate, w_up, w_down)
    ]

    own = restore(tokens, expert_ids.T, affinity.T)
    near = [(move(own[h], h, 1), move(own[h], h, -1)) for h in range(2)]
    gathered = []
    for h in range(2):
        back, ahead = near[h]
        piece1 = move(back[:, : half // 2], h, 1)
        piece2 = move(ahead[:, half // 2 :], h, -1)
        gathered.append((own[h], back, ahead, piece1, piece2))
    sent = pick_slots(targets, gathered, side)
    table = weights_of_slots(targets, gathered, side)

    def across(rings, sign):
        return [
            [v if o == 0 else move(v, 1 - h, sign * o) for o, v in zip(OFFSETS, rings[h])]
            for h in range(2)
        ]

    parts = [across(expert(across(rings, 1), gates, ups, downs), -1) for rings in sent]
    sums = partial_sums(table, parts)
    joined = add_pieces(
        [
            (back, ahead, move(piece1, h, 1), move(piece2, h, -1))
            for h, (_own, back, ahead, piece1, piece2) in enumerate(sums)
        ]
    )
    return final_sum(
        [
            (sums[h][0], move(joined[h][0], h, -1), move(joined[h][1], h, 1))
            for h in range(2)
        ]
    )


def solution(mesh):
    rows = P(("dp", "ep"), None)
    weights = P("ep", None, None)
    return jax.shard_map(
        on_device,
        mesh=mesh,
        in_specs=(rows, rows, rows, weights, weights, weights),
        out_specs=rows,
        check_vma=False,
    )
```

```python
import functools
import jax
import jax.numpy as jnp
from jax import lax
from jax.experimental import pallas as pl
from jax.experimental.pallas import tpu as pltpu
from jax.sharding import PartitionSpec as P

TOP = 2
BLOCK = 16
LANES = 128
CHUNKS = 2
PIECES = 7
VMEM_BYTES = 56 * 1024 * 1024


def iota(shape, dim):
    return lax.broadcasted_iota(jnp.int32, shape, dim)


def halves(value):
    upper = value.astype(jnp.bfloat16)
    return upper, (value - upper.astype(jnp.float32)).astype(jnp.bfloat16)


def ones_where(hit):
    return hit.astype(jnp.float32).astype(jnp.bfloat16)


def times(a, b):
    return jnp.dot(a, b, preferred_element_type=jnp.float32)


def slot_keys(turned_ids_ref, experts):
    count = turned_ids_ref.shape[1]
    row = iota((experts, count), 0)
    hit = turned_ids_ref[0:1, :] == row
    for k in range(1, TOP):
        hit = hit | (turned_ids_ref[k : k + 1, :] == row)
    earlier = ones_where(iota((count, count), 0) < iota((count, count), 1))
    rank = times(ones_where(hit), earlier)
    return jnp.where(hit, rank, -1.0).astype(jnp.bfloat16)


def restored_rows(tokens, gather, spread, spread3):
    x = tokens.astype(jnp.float32)
    width = x.shape[1]
    tops = []
    for at in range(0, width, LANES):
        top = jnp.abs(x[:, at : at + LANES])
        for step in (1, 2, 4, 8):
            top = jnp.maximum(top, pltpu.roll(top, LANES - step, 1))
        tops.append(top.astype(jnp.bfloat16))
    largest = times(jnp.concatenate(tops, axis=1), gather)
    scale = (jnp.maximum(largest, 0.25) / 9.0).astype(jnp.bfloat16)
    inverse = 1.0 / scale.astype(jnp.float32)
    first, rest = halves(inverse)
    second, third = halves(inverse - first.astype(jnp.float32))
    inverse = times(jnp.concatenate([first, second, third], axis=1), spread3)
    scale = times(scale, spread)
    payload = jnp.clip(x * inverse, -6.0, 6.0).astype(jnp.bfloat16).astype(jnp.float32)
    return (payload * scale).astype(jnp.bfloat16)


def pick_kernel(experts, chunk, ids_ref, tokens_ref, out_ref, tokens, rows_out, pick, got, put):
    count, width = tokens.shape
    rows = rows_out.shape[0]
    each = rows // experts
    pieces = got.shape[0]
    wide = width // pieces

    def loaded(i):
        part = (slice(None), pl.ds(i * wide, wide))
        return pltpu.make_async_copy(tokens_ref.at[part], tokens.at[part], got.at[i])

    def stored(i):
        part = (slice(None), pl.ds(i * wide, wide))
        return pltpu.make_async_copy(rows_out.at[part], out_ref.at[part], put.at[i])

    for i in range(pieces):
        loaded(i).start()
    key = slot_keys(ids_ref, experts)
    all_keys = times(ones_where(iota((rows, experts), 0) // each == iota((rows, experts), 1)), key)
    place = (iota((rows, count), 0) % each + each * chunk).astype(jnp.float32)
    pick[...] = ones_where(all_keys == place)
    for i in range(pieces):
        loaded(i).wait()
        part = tokens[:, i * wide : (i + 1) * wide]
        rows_out[:, i * wide : (i + 1) * wide] = times(pick[...], part).astype(jnp.bfloat16)
        stored(i).start()
    for i in range(pieces):
        stored(i).wait()


def slots_of_tokens(tokens, turned_ids, experts, slots, chunk):
    count, width = tokens.shape
    rows = experts * slots // CHUNKS
    return pl.pallas_call(
        functools.partial(pick_kernel, experts, chunk),
        name="pick_slots",
        out_shape=jax.ShapeDtypeStruct((rows, width), jnp.bfloat16),
        in_specs=[pl.BlockSpec(memory_space=pltpu.VMEM), pl.BlockSpec(memory_space=pl.ANY)],
        out_specs=pl.BlockSpec(memory_space=pl.ANY),
        scratch_shapes=[
            pltpu.VMEM((count, width), jnp.bfloat16),
            pltpu.VMEM((rows, width), jnp.bfloat16),
            pltpu.VMEM((rows, count), jnp.bfloat16),
            pltpu.SemaphoreType.DMA((PIECES,)),
            pltpu.SemaphoreType.DMA((PIECES,)),
        ],
        compiler_params=pltpu.CompilerParams(vmem_limit_bytes=VMEM_BYTES),
    )(turned_ids, tokens)


def expert_kernel(
    steps,
    x_ref,
    g0,
    g1,
    u0,
    u1,
    d0,
    d1,
    out_ref,
    gate0,
    gate1,
    up0,
    up1,
    hid0,
    hid1,
    gather,
    spread,
    spread3,
):
    step = pl.program_id(0)
    pairs = ((gate0, g0), (gate1, g1), (up0, u0), (up1, u1))

    @pl.when(step == 0)
    def _():
        for total, _w in pairs:
            total[...] = jnp.zeros_like(total)
        width, blocks = gather.shape
        gather[...] = ones_where(iota((width, blocks), 0) == BLOCK * iota((width, blocks), 1))
        spread[...] = ones_where(iota((blocks, width), 1) // BLOCK == iota((blocks, width), 0))
        for j in range(3):
            spread3[j * blocks : (j + 1) * blocks, :] = spread[...]

    @pl.when(step < steps)
    def _():
        x = restored_rows(x_ref[...], gather[...], spread[...], spread3[...])
        for total, w in pairs:
            total[...] += jnp.dot(x, w[...], preferred_element_type=jnp.float32)

    @pl.when(step == steps - 1)
    def _():
        for hid, gate, up in ((hid0, gate0, up0), (hid1, gate1, up1)):
            v = gate[...]
            hid[...] = (v / (1.0 + jnp.exp(-v)) * up[...]).astype(jnp.bfloat16)

    @pl.when(step >= steps)
    def _():
        out_ref[...] = (
            jnp.dot(hid0[...], d0[...], preferred_element_type=jnp.float32)
            + jnp.dot(hid1[...], d1[...], preferred_element_type=jnp.float32)
        ).astype(jnp.bfloat16)


def expert(rows, gates, ups, downs):
    count, width = rows.shape
    half = gates[0].shape[-1]
    wide = 1024
    steps = width // wide
    first = lambda s: jnp.minimum(s, steps - 1)
    second = lambda s: jnp.maximum(s - steps, 0)
    into = pl.BlockSpec((None, wide, half), lambda s: (0, first(s), 0))
    out_of = pl.BlockSpec((None, half, wide), lambda s: (0, 0, second(s)))
    return pl.pallas_call(
        functools.partial(expert_kernel, steps),
        name="expert_rows",
        out_shape=jax.ShapeDtypeStruct((count, width), jnp.bfloat16),
        grid=(2 * steps,),
        in_specs=[pl.BlockSpec((count, wide), lambda s: (0, first(s)))] + [into] * 4 + [out_of] * 2,
        out_specs=pl.BlockSpec((count, wide), lambda s: (0, second(s))),
        scratch_shapes=[pltpu.VMEM((count, half), jnp.float32)] * 4
        + [pltpu.VMEM((count, half), jnp.bfloat16)] * 2
        + [
            pltpu.VMEM((wide, wide // BLOCK), jnp.bfloat16),
            pltpu.VMEM((wide // BLOCK, wide), jnp.bfloat16),
            pltpu.VMEM((3 * wide // BLOCK, wide), jnp.bfloat16),
        ],
        compiler_params=pltpu.CompilerParams(
            dimension_semantics=("arbitrary",), vmem_limit_bytes=VMEM_BYTES
        ),
        cost_estimate=pl.CostEstimate(
            flops=count * width * half * 12,
            transcendentals=count * half * 2,
            bytes_accessed=width * half * 12 + count * width * 4,
        ),
    )(rows, *gates, *ups, *downs)


def table_kernel(experts, chunks, ids_ref, affinity_ref, out_ref):
    count = ids_ref.shape[1]
    rows = out_ref.shape[2]
    each = rows // experts
    key = slot_keys(ids_ref, experts)
    total = affinity_ref[0:1, :]
    for k in range(1, TOP):
        total = total + affinity_ref[k : k + 1, :]
    row = iota((experts, count), 0)
    weight = jnp.zeros((experts, count), jnp.float32)
    for k in range(TOP):
        share = affinity_ref[k : k + 1, :] / total
        weight = jnp.where(ids_ref[k : k + 1, :] == row, share, weight)
    same = ones_where(iota((count, count), 0) == iota((count, count), 1))
    spread = ones_where(iota((experts, rows), 1) // each == iota((experts, rows), 0))

    def by_token(value):
        turned = lax.dot_general(
            same, value, (((1,), (1,)), ((), ())), preferred_element_type=jnp.float32
        )
        return times(turned.astype(jnp.bfloat16), spread)

    wide = by_token(key)
    upper, lower = [by_token(part) for part in halves(weight)]
    place = (iota((count, rows), 1) % each).astype(jnp.float32)
    for j in range(chunks):
        hit = wide == place + float(each * j)
        out_ref[j, 0:count, :] = jnp.where(hit, upper, 0.0).astype(jnp.bfloat16)
        out_ref[j, count : 2 * count, :] = jnp.where(hit, lower, 0.0).astype(jnp.bfloat16)


def weights_of_slots(turned_ids, turned_affinity, experts, slots, chunks):
    count = turned_ids.shape[1]
    rows = experts * slots // chunks
    return pl.pallas_call(
        functools.partial(table_kernel, experts, chunks),
        name="slot_weights",
        out_shape=jax.ShapeDtypeStruct((chunks, 2 * count, rows), jnp.bfloat16),
    )(turned_ids, turned_affinity)


def mix_kernel(chunks, table_ref, *rest):
    in_refs, out_ref = rest[:chunks], rest[chunks]
    values, mixed, got, put = rest[chunks + 1 :]
    count, width = mixed.shape
    rows = values.shape[1]
    pieces = put.shape[0]
    wide = width // pieces

    def loaded(j, i):
        part = (slice(None), pl.ds(i * wide, wide))
        return pltpu.make_async_copy(in_refs[j].at[part], values.at[j].at[part], got.at[j, i])

    def stored(i):
        part = (slice(None), pl.ds(i * wide, wide))
        return pltpu.make_async_copy(mixed.at[part], out_ref.at[part], put.at[i])

    for i in range(pieces):
        for j in range(chunks):
            loaded(j, i).start()
    for i in range(pieces):
        total = None
        for j in range(chunks):
            loaded(j, i).wait()
            part = times(table_ref[j], values[j, :, i * wide : (i + 1) * wide])
            total = part if total is None else total + part
        total = total[:count] + total[count:]
        mixed[:, i * wide : (i + 1) * wide] = total.astype(jnp.bfloat16)
        stored(i).start()
    for i in range(pieces):
        stored(i).wait()


def mix(table, parts):
    chunks, count, rows = table.shape
    count //= 2
    width = parts[0].shape[1]
    anywhere = pl.BlockSpec(memory_space=pl.ANY)
    return pl.pallas_call(
        functools.partial(mix_kernel, chunks),
        name="mix_slots",
        out_shape=jax.ShapeDtypeStruct((count, width), jnp.bfloat16),
        in_specs=[pl.BlockSpec(memory_space=pltpu.VMEM)] + [anywhere] * chunks,
        out_specs=anywhere,
        scratch_shapes=[
            pltpu.VMEM((chunks, rows, width), jnp.bfloat16),
            pltpu.VMEM((count, width), jnp.bfloat16),
            pltpu.SemaphoreType.DMA((chunks, PIECES)),
            pltpu.SemaphoreType.DMA((PIECES,)),
        ],
        compiler_params=pltpu.CompilerParams(vmem_limit_bytes=VMEM_BYTES),
    )(table, *parts)


def exchange(rows, devices):
    count, width = rows.shape
    chips = devices // 2
    groups = [list(range(core, devices, 2)) for core in range(2)]
    return lax.all_to_all(
        rows.reshape(chips, count // chips, width),
        "ep",
        split_axis=0,
        concat_axis=0,
        axis_index_groups=groups,
        tiled=True,
    ).reshape(count, width)


def on_device(tokens, expert_ids, affinity, w_gate, w_up, w_down):
    devices = lax.axis_size("ep")
    experts = devices // 2
    slots = 2 * tokens.shape[0] * TOP // experts
    pairs = [(s, s ^ 1) for s in range(devices)]
    gates, ups, downs = [(w, lax.ppermute(w, "ep", pairs)) for w in (w_gate, w_up, w_down)]
    turned_ids = expert_ids.T
    table = weights_of_slots(turned_ids, affinity.T, experts, slots, CHUNKS)
    parts = []
    for chunk in range(CHUNKS):
        rows = exchange(slots_of_tokens(tokens, turned_ids, experts, slots, chunk), devices)
        parts.append(exchange(expert(rows, gates, ups, downs), devices))
    return mix(table, parts)


def solution(mesh):
    rows = P(("dp", "ep"), None)
    weights = P("ep", None, None)
    return jax.shard_map(
        on_device,
        mesh=mesh,
        in_specs=(rows, rows, rows, weights, weights, weights),
        out_specs=rows,
        check_vma=False,
    )
```

```python
import functools
import jax
import jax.numpy as jnp
from jax import lax
from jax.experimental import pallas as pl
from jax.experimental.pallas import tpu as pltpu
from jax.sharding import PartitionSpec as P

TOP = 2
BLOCK = 16
LANES = 128
CHUNKS = 2
PIECES = 7
VMEM_BYTES = 56 * 1024 * 1024


def iota(shape, dim):
    return lax.broadcasted_iota(jnp.int32, shape, dim)


def halves(value):
    upper = value.astype(jnp.bfloat16)
    return upper, (value - upper.astype(jnp.float32)).astype(jnp.bfloat16)


def ones_where(hit):
    return hit.astype(jnp.float32).astype(jnp.bfloat16)


def times(a, b):
    return jnp.dot(a, b, preferred_element_type=jnp.float32)


def slot_keys(turned_ids_ref, experts):
    count = turned_ids_ref.shape[1]
    row = iota((experts, count), 0)
    hit = turned_ids_ref[0:1, :] == row
    for k in range(1, TOP):
        hit = hit | (turned_ids_ref[k : k + 1, :] == row)
    earlier = ones_where(iota((count, count), 0) < iota((count, count), 1))
    rank = times(ones_where(hit), earlier)
    return jnp.where(hit, rank, -1.0).astype(jnp.bfloat16)


def restored_rows(tokens, gather, spread, spread3):
    x = tokens.astype(jnp.float32)
    width = x.shape[1]
    tops = []
    for at in range(0, width, LANES):
        top = jnp.abs(x[:, at : at + LANES])
        for step in (1, 2, 4, 8):
            top = jnp.maximum(top, pltpu.roll(top, LANES - step, 1))
        tops.append(top.astype(jnp.bfloat16))
    largest = times(jnp.concatenate(tops, axis=1), gather)
    scale = (jnp.maximum(largest, 0.25) / 9.0).astype(jnp.bfloat16)
    inverse = 1.0 / scale.astype(jnp.float32)
    first, rest = halves(inverse)
    second, third = halves(inverse - first.astype(jnp.float32))
    inverse = times(jnp.concatenate([first, second, third], axis=1), spread3)
    scale = times(scale, spread)
    payload = jnp.clip(x * inverse, -6.0, 6.0).astype(jnp.bfloat16).astype(jnp.float32)
    return (payload * scale).astype(jnp.bfloat16)


def pick_kernel(experts, chunk, ids_ref, tokens_ref, out_ref, tokens, rows_out, pick, got, put):
    count, width = tokens.shape
    rows = rows_out.shape[0]
    each = rows // experts
    pieces = got.shape[0]
    wide = width // pieces

    def loaded(i):
        part = (slice(None), pl.ds(i * wide, wide))
        return pltpu.make_async_copy(tokens_ref.at[part], tokens.at[part], got.at[i])

    def stored(i):
        part = (slice(None), pl.ds(i * wide, wide))
        return pltpu.make_async_copy(rows_out.at[part], out_ref.at[part], put.at[i])

    for i in range(pieces):
        loaded(i).start()
    key = slot_keys(ids_ref, experts)
    all_keys = times(ones_where(iota((rows, experts), 0) // each == iota((rows, experts), 1)), key)
    place = (iota((rows, count), 0) % each + each * chunk).astype(jnp.float32)
    pick[...] = ones_where(all_keys == place)
    for i in range(pieces):
        loaded(i).wait()
        part = tokens[:, i * wide : (i + 1) * wide]
        rows_out[:, i * wide : (i + 1) * wide] = times(pick[...], part).astype(jnp.bfloat16)
        stored(i).start()
    for i in range(pieces):
        stored(i).wait()


def slots_of_tokens(tokens, turned_ids, experts, slots, chunk):
    count, width = tokens.shape
    rows = experts * slots // CHUNKS
    return pl.pallas_call(
        functools.partial(pick_kernel, experts, chunk),
        name="pick_slots",
        out_shape=jax.ShapeDtypeStruct((rows, width), jnp.bfloat16),
        in_specs=[pl.BlockSpec(memory_space=pltpu.VMEM), pl.BlockSpec(memory_space=pl.ANY)],
        out_specs=pl.BlockSpec(memory_space=pl.ANY),
        scratch_shapes=[
            pltpu.VMEM((count, width), jnp.bfloat16),
            pltpu.VMEM((rows, width), jnp.bfloat16),
            pltpu.VMEM((rows, count), jnp.bfloat16),
            pltpu.SemaphoreType.DMA((PIECES,)),
            pltpu.SemaphoreType.DMA((PIECES,)),
        ],
        compiler_params=pltpu.CompilerParams(vmem_limit_bytes=VMEM_BYTES),
    )(turned_ids, tokens)


def expert_kernel(
    steps,
    x_ref,
    g0,
    g1,
    u0,
    u1,
    d0,
    d1,
    out_ref,
    gate0,
    gate1,
    up0,
    up1,
    hid0,
    hid1,
    gather,
    spread,
    spread3,
):
    step = pl.program_id(0)
    pairs = ((gate0, g0), (gate1, g1), (up0, u0), (up1, u1))

    @pl.when(step == 0)
    def _():
        for total, _w in pairs:
            total[...] = jnp.zeros_like(total)
        width, blocks = gather.shape
        gather[...] = ones_where(iota((width, blocks), 0) == BLOCK * iota((width, blocks), 1))
        spread[...] = ones_where(iota((blocks, width), 1) // BLOCK == iota((blocks, width), 0))
        for j in range(3):
            spread3[j * blocks : (j + 1) * blocks, :] = spread[...]

    @pl.when(step < steps)
    def _():
        x = restored_rows(x_ref[...], gather[...], spread[...], spread3[...])
        for total, w in pairs:
            total[...] += jnp.dot(x, w[...], preferred_element_type=jnp.float32)

    @pl.when(step == steps - 1)
    def _():
        for hid, gate, up in ((hid0, gate0, up0), (hid1, gate1, up1)):
            v = gate[...]
            hid[...] = (v / (1.0 + jnp.exp(-v)) * up[...]).astype(jnp.bfloat16)

    @pl.when(step >= steps)
    def _():
        out_ref[...] = (
            jnp.dot(hid0[...], d0[...], preferred_element_type=jnp.float32)
            + jnp.dot(hid1[...], d1[...], preferred_element_type=jnp.float32)
        ).astype(jnp.bfloat16)


def expert(rows, gates, ups, downs):
    count, width = rows.shape
    half = gates.shape[-1]
    wide = 1024
    steps = width // wide
    first = lambda s: jnp.minimum(s, steps - 1)
    second = lambda s: jnp.maximum(s - steps, 0)
    into = [pl.BlockSpec((None, wide, half), lambda s, c=c: (c, first(s), 0)) for c in range(2)]
    out_of = [pl.BlockSpec((None, half, wide), lambda s, c=c: (c, 0, second(s))) for c in range(2)]
    return pl.pallas_call(
        functools.partial(expert_kernel, steps),
        name="expert_rows",
        out_shape=jax.ShapeDtypeStruct((count, width), jnp.bfloat16),
        grid=(2 * steps,),
        in_specs=[pl.BlockSpec((count, wide), lambda s: (0, first(s)))] + into * 2 + out_of,
        out_specs=pl.BlockSpec((count, wide), lambda s: (0, second(s))),
        scratch_shapes=[pltpu.VMEM((count, half), jnp.float32)] * 4
        + [pltpu.VMEM((count, half), jnp.bfloat16)] * 2
        + [
            pltpu.VMEM((wide, wide // BLOCK), jnp.bfloat16),
            pltpu.VMEM((wide // BLOCK, wide), jnp.bfloat16),
            pltpu.VMEM((3 * wide // BLOCK, wide), jnp.bfloat16),
        ],
        compiler_params=pltpu.CompilerParams(
            dimension_semantics=("arbitrary",), vmem_limit_bytes=VMEM_BYTES
        ),
        cost_estimate=pl.CostEstimate(
            flops=count * width * half * 12,
            transcendentals=count * half * 2,
            bytes_accessed=width * half * 12 + count * width * 4,
        ),
    )(rows, gates, gates, ups, ups, downs, downs)


def table_kernel(experts, chunks, ids_ref, affinity_ref, out_ref):
    count = ids_ref.shape[1]
    rows = out_ref.shape[2]
    each = rows // experts
    key = slot_keys(ids_ref, experts)
    total = affinity_ref[0:1, :]
    for k in range(1, TOP):
        total = total + affinity_ref[k : k + 1, :]
    row = iota((experts, count), 0)
    weight = jnp.zeros((experts, count), jnp.float32)
    for k in range(TOP):
        share = affinity_ref[k : k + 1, :] / total
        weight = jnp.where(ids_ref[k : k + 1, :] == row, share, weight)
    same = ones_where(iota((count, count), 0) == iota((count, count), 1))
    spread = ones_where(iota((experts, rows), 1) // each == iota((experts, rows), 0))

    def by_token(value):
        turned = lax.dot_general(
            same, value, (((1,), (1,)), ((), ())), preferred_element_type=jnp.float32
        )
        return times(turned.astype(jnp.bfloat16), spread)

    wide = by_token(key)
    upper, lower = [by_token(part) for part in halves(weight)]
    place = (iota((count, rows), 1) % each).astype(jnp.float32)
    for j in range(chunks):
        hit = wide == place + float(each * j)
        out_ref[j, 0:count, :] = jnp.where(hit, upper, 0.0).astype(jnp.bfloat16)
        out_ref[j, count : 2 * count, :] = jnp.where(hit, lower, 0.0).astype(jnp.bfloat16)


def weights_of_slots(turned_ids, turned_affinity, experts, slots, chunks):
    count = turned_ids.shape[1]
    rows = experts * slots // chunks
    return pl.pallas_call(
        functools.partial(table_kernel, experts, chunks),
        name="slot_weights",
        out_shape=jax.ShapeDtypeStruct((chunks, 2 * count, rows), jnp.bfloat16),
    )(turned_ids, turned_affinity)


def mix_kernel(chunks, table_ref, *rest):
    in_refs, out_ref = rest[:chunks], rest[chunks]
    values, mixed, got, put = rest[chunks + 1 :]
    count, width = mixed.shape
    rows = values.shape[1]
    pieces = put.shape[0]
    wide = width // pieces

    def loaded(j, i):
        part = (slice(None), pl.ds(i * wide, wide))
        return pltpu.make_async_copy(in_refs[j].at[part], values.at[j].at[part], got.at[j, i])

    def stored(i):
        part = (slice(None), pl.ds(i * wide, wide))
        return pltpu.make_async_copy(mixed.at[part], out_ref.at[part], put.at[i])

    for i in range(pieces):
        for j in range(chunks):
            loaded(j, i).start()
    for i in range(pieces):
        total = None
        for j in range(chunks):
            loaded(j, i).wait()
            part = times(table_ref[j], values[j, :, i * wide : (i + 1) * wide])
            total = part if total is None else total + part
        total = total[:count] + total[count:]
        mixed[:, i * wide : (i + 1) * wide] = total.astype(jnp.bfloat16)
        stored(i).start()
    for i in range(pieces):
        stored(i).wait()


def mix(table, parts):
    chunks, count, rows = table.shape
    count //= 2
    width = parts[0].shape[1]
    anywhere = pl.BlockSpec(memory_space=pl.ANY)
    return pl.pallas_call(
        functools.partial(mix_kernel, chunks),
        name="mix_slots",
        out_shape=jax.ShapeDtypeStruct((count, width), jnp.bfloat16),
        in_specs=[pl.BlockSpec(memory_space=pltpu.VMEM)] + [anywhere] * chunks,
        out_specs=anywhere,
        scratch_shapes=[
            pltpu.VMEM((chunks, rows, width), jnp.bfloat16),
            pltpu.VMEM((count, width), jnp.bfloat16),
            pltpu.SemaphoreType.DMA((chunks, PIECES)),
            pltpu.SemaphoreType.DMA((PIECES,)),
        ],
        compiler_params=pltpu.CompilerParams(vmem_limit_bytes=VMEM_BYTES),
    )(table, *parts)


def exchange(rows, devices):
    count, width = rows.shape
    split = rows.reshape(devices, count // devices, width)
    return lax.all_to_all(split, "ep", split_axis=0, concat_axis=0, tiled=True).reshape(
        count, width
    )


def on_device(tokens, expert_ids, affinity, w_gate, w_up, w_down):
    devices = lax.axis_size("ep")
    experts = devices // 2
    slots = 2 * tokens.shape[0] * TOP // experts
    mates = [[s, s + 1] for s in range(0, devices, 2)]
    gates, ups, downs = [
        lax.all_gather(w, "ep", axis_index_groups=mates, axis=0, tiled=True)
        for w in (w_gate, w_up, w_down)
    ]
    turned_ids = expert_ids.T
    table = weights_of_slots(turned_ids, affinity.T, experts, slots, CHUNKS)
    parts = []
    for chunk in range(CHUNKS):
        rows = exchange(slots_of_tokens(tokens, turned_ids, experts, slots, chunk), devices)
        parts.append(exchange(expert(rows, gates, ups, downs), devices))
    return mix(table, parts)


def solution(mesh):
    rows = P(("dp", "ep"), None)
    weights = P("ep", None, None)
    return jax.shard_map(
        on_device,
        mesh=mesh,
        in_specs=(rows, rows, rows, weights, weights, weights),
        out_specs=rows,
        check_vma=False,
    )
```

```python
import functools
import jax
import jax.numpy as jnp
from jax import lax
from jax.experimental import pallas as pl
from jax.experimental.pallas import tpu as pltpu
from jax.sharding import PartitionSpec as P

TOP = 2
BLOCK = 16
LANES = 128
CHUNKS = 2
PIECES = 7
VMEM_BYTES = 56 * 1024 * 1024


def iota(shape, dim):
    return lax.broadcasted_iota(jnp.int32, shape, dim)


def halves(value):
    upper = value.astype(jnp.bfloat16)
    return upper, (value - upper.astype(jnp.float32)).astype(jnp.bfloat16)


def ones_where(hit):
    return hit.astype(jnp.float32).astype(jnp.bfloat16)


def times(a, b):
    return jnp.dot(a, b, preferred_element_type=jnp.float32)


def slot_keys(turned_ids_ref, experts):
    count = turned_ids_ref.shape[1]
    row = iota((experts, count), 0)
    hit = turned_ids_ref[0:1, :] == row
    for k in range(1, TOP):
        hit = hit | (turned_ids_ref[k : k + 1, :] == row)
    earlier = ones_where(iota((count, count), 0) < iota((count, count), 1))
    rank = times(ones_where(hit), earlier)
    return jnp.where(hit, rank, -1.0).astype(jnp.bfloat16)


def restored_rows(tokens, gather, spread, spread3):
    x = tokens.astype(jnp.float32)
    width = x.shape[1]
    tops = []
    for at in range(0, width, LANES):
        top = jnp.abs(x[:, at : at + LANES])
        for step in (1, 2, 4, 8):
            top = jnp.maximum(top, pltpu.roll(top, LANES - step, 1))
        tops.append(top.astype(jnp.bfloat16))
    largest = times(jnp.concatenate(tops, axis=1), gather)
    scale = (jnp.maximum(largest, 0.25) / 9.0).astype(jnp.bfloat16)
    inverse = 1.0 / scale.astype(jnp.float32)
    first, rest = halves(inverse)
    second, third = halves(inverse - first.astype(jnp.float32))
    inverse = times(jnp.concatenate([first, second, third], axis=1), spread3)
    scale = times(scale, spread)
    payload = jnp.clip(x * inverse, -6.0, 6.0).astype(jnp.bfloat16).astype(jnp.float32)
    return (payload * scale).astype(jnp.bfloat16)


def pick_kernel(experts, chunk, ids_ref, tokens_ref, out_ref, tokens, rows_out, pick, got, put):
    count, width = tokens.shape
    rows = rows_out.shape[0]
    each = rows // experts
    pieces = got.shape[0]
    wide = width // pieces

    def loaded(i):
        part = (slice(None), pl.ds(i * wide, wide))
        return pltpu.make_async_copy(tokens_ref.at[part], tokens.at[part], got.at[i])

    def stored(i):
        part = (slice(None), pl.ds(i * wide, wide))
        return pltpu.make_async_copy(rows_out.at[part], out_ref.at[part], put.at[i])

    for i in range(pieces):
        loaded(i).start()
    key = slot_keys(ids_ref, experts)
    all_keys = times(ones_where(iota((rows, experts), 0) // each == iota((rows, experts), 1)), key)
    place = (iota((rows, count), 0) % each + each * chunk).astype(jnp.float32)
    pick[...] = ones_where(all_keys == place)
    for i in range(pieces):
        loaded(i).wait()
        part = tokens[:, i * wide : (i + 1) * wide]
        rows_out[:, i * wide : (i + 1) * wide] = times(pick[...], part).astype(jnp.bfloat16)
        stored(i).start()
    for i in range(pieces):
        stored(i).wait()


def slots_of_tokens(tokens, turned_ids, experts, slots, chunk):
    count, width = tokens.shape
    rows = experts * slots // CHUNKS
    return pl.pallas_call(
        functools.partial(pick_kernel, experts, chunk),
        name="pick_slots",
        out_shape=jax.ShapeDtypeStruct((rows, width), jnp.bfloat16),
        in_specs=[pl.BlockSpec(memory_space=pltpu.VMEM), pl.BlockSpec(memory_space=pl.ANY)],
        out_specs=pl.BlockSpec(memory_space=pl.ANY),
        scratch_shapes=[
            pltpu.VMEM((count, width), jnp.bfloat16),
            pltpu.VMEM((rows, width), jnp.bfloat16),
            pltpu.VMEM((rows, count), jnp.bfloat16),
            pltpu.SemaphoreType.DMA((PIECES,)),
            pltpu.SemaphoreType.DMA((PIECES,)),
        ],
        compiler_params=pltpu.CompilerParams(vmem_limit_bytes=VMEM_BYTES),
    )(turned_ids, tokens)


def hidden_kernel(x_ref, g0, g1, u0, u1, out_ref, gate0, gate1, up0, up1, gather, spread, spread3):
    step = pl.program_id(0)
    pairs = ((gate0, g0), (gate1, g1), (up0, u0), (up1, u1))
    half = gate0.shape[1]

    @pl.when(step == 0)
    def _():
        for total, _w in pairs:
            total[...] = jnp.zeros_like(total)
        width, blocks = gather.shape
        gather[...] = ones_where(iota((width, blocks), 0) == BLOCK * iota((width, blocks), 1))
        spread[...] = ones_where(iota((blocks, width), 1) // BLOCK == iota((blocks, width), 0))
        for j in range(3):
            spread3[j * blocks : (j + 1) * blocks, :] = spread[...]

    x = restored_rows(x_ref[...], gather[...], spread[...], spread3[...])
    for total, w in pairs:
        total[...] += times(x, w[...])

    @pl.when(step == pl.num_programs(0) - 1)
    def _():
        for at, gate, up in ((0, gate0, up0), (half, gate1, up1)):
            v = gate[...]
            out_ref[:, at : at + half] = (v / (1.0 + jnp.exp(-v)) * up[...]).astype(jnp.bfloat16)


def hidden_units(rows, gates, ups):
    count, width = rows.shape
    half = gates.shape[-1]
    wide = 1024
    blocks = wide // BLOCK
    into = [pl.BlockSpec((None, wide, half), lambda s, c=c: (c, s, 0)) for c in range(2)]
    return pl.pallas_call(
        hidden_kernel,
        name="hidden_units",
        out_shape=jax.ShapeDtypeStruct((count, 2 * half), jnp.bfloat16),
        grid=(width // wide,),
        in_specs=[pl.BlockSpec((count, wide), lambda s: (0, s))] + into * 2,
        out_specs=pl.BlockSpec((count, 2 * half), lambda s: (0, 0)),
        scratch_shapes=[pltpu.VMEM((count, half), jnp.float32)] * 4
        + [
            pltpu.VMEM((wide, blocks), jnp.bfloat16),
            pltpu.VMEM((blocks, wide), jnp.bfloat16),
            pltpu.VMEM((3 * blocks, wide), jnp.bfloat16),
        ],
        compiler_params=pltpu.CompilerParams(
            dimension_semantics=("arbitrary",), vmem_limit_bytes=VMEM_BYTES
        ),
        cost_estimate=pl.CostEstimate(
            flops=count * width * half * 8,
            transcendentals=count * half * 2,
            bytes_accessed=width * half * 8 + count * width * 2,
        ),
    )(rows, gates, gates, ups, ups)


def down_kernel(hidden_ref, d0, d1, out_ref):
    half = d0.shape[0]
    hidden = hidden_ref[...]
    out_ref[...] = (times(hidden[:, :half], d0[...]) + times(hidden[:, half:], d1[...])).astype(
        jnp.bfloat16
    )


def down_rows(hidden, downs):
    count = hidden.shape[0]
    _, half, width = downs.shape
    wide = 1024
    out_of = [pl.BlockSpec((None, half, wide), lambda s, c=c: (c, 0, s)) for c in range(2)]
    return pl.pallas_call(
        down_kernel,
        name="down_rows",
        out_shape=jax.ShapeDtypeStruct((count, width), jnp.bfloat16),
        grid=(width // wide,),
        in_specs=[pl.BlockSpec(hidden.shape, lambda s: (0, 0))] + out_of,
        out_specs=pl.BlockSpec((count, wide), lambda s: (0, s)),
        compiler_params=pltpu.CompilerParams(
            dimension_semantics=("arbitrary",), vmem_limit_bytes=VMEM_BYTES
        ),
        cost_estimate=pl.CostEstimate(
            flops=count * width * half * 4,
            transcendentals=0,
            bytes_accessed=width * half * 4 + count * width * 2,
        ),
    )(hidden, downs, downs)


def table_kernel(experts, chunks, ids_ref, affinity_ref, *out_refs):
    count = ids_ref.shape[1]
    rows = out_refs[0].shape[1]
    each = rows // experts
    key = slot_keys(ids_ref, experts)
    total = affinity_ref[0:1, :]
    for k in range(1, TOP):
        total = total + affinity_ref[k : k + 1, :]
    row = iota((experts, count), 0)
    weight = jnp.zeros((experts, count), jnp.float32)
    for k in range(TOP):
        share = affinity_ref[k : k + 1, :] / total
        weight = jnp.where(ids_ref[k : k + 1, :] == row, share, weight)
    same = ones_where(iota((count, count), 0) == iota((count, count), 1))
    spread = ones_where(iota((experts, rows), 1) // each == iota((experts, rows), 0))

    def by_token(value):
        turned = lax.dot_general(
            same, value, (((1,), (1,)), ((), ())), preferred_element_type=jnp.float32
        )
        return times(turned.astype(jnp.bfloat16), spread)

    wide = by_token(key)
    upper, lower = [by_token(part) for part in halves(weight)]
    place = (iota((count, rows), 1) % each).astype(jnp.float32)
    for j in range(chunks):
        hit = wide == place + float(each * j)
        out_refs[j][0:count, :] = jnp.where(hit, upper, 0.0).astype(jnp.bfloat16)
        out_refs[j][count : 2 * count, :] = jnp.where(hit, lower, 0.0).astype(jnp.bfloat16)


def weights_of_slots(turned_ids, turned_affinity, experts, slots, chunks):
    count = turned_ids.shape[1]
    rows = experts * slots // chunks
    return pl.pallas_call(
        functools.partial(table_kernel, experts, chunks),
        name="slot_weights",
        out_shape=[jax.ShapeDtypeStruct((2 * count, rows), jnp.bfloat16)] * chunks,
    )(turned_ids, turned_affinity)


def mix_kernel(table_ref, in_ref, *rest):
    known_refs, out_ref = rest[:-5], rest[-5]
    values, mixed, got, put = rest[-4:]
    count, width = mixed.shape
    pieces = put.shape[0]
    wide = width // pieces

    def part(i):
        return (slice(None), pl.ds(i * wide, wide))

    def loaded(i):
        return pltpu.make_async_copy(in_ref.at[part(i)], values.at[part(i)], got.at[i])

    def stored(i):
        return pltpu.make_async_copy(mixed.at[part(i)], out_ref.at[part(i)], put.at[i])

    for i in range(pieces):
        loaded(i).start()
    for i in range(pieces):
        loaded(i).wait()
        both = times(table_ref[...], values[:, i * wide : (i + 1) * wide])
        total = both[:count] + both[count:]
        for known in known_refs:
            total = total + known[:, i * wide : (i + 1) * wide]
        mixed[:, i * wide : (i + 1) * wide] = total.astype(mixed.dtype)
        stored(i).start()
    for i in range(pieces):
        stored(i).wait()


def mix(table, rows, known, dtype):
    count = table.shape[0] // 2
    slots, width = rows.shape
    anywhere = pl.BlockSpec(memory_space=pl.ANY)
    vmem = pl.BlockSpec(memory_space=pltpu.VMEM)
    return pl.pallas_call(
        mix_kernel,
        name="mix_slots",
        out_shape=jax.ShapeDtypeStruct((count, width), dtype),
        in_specs=[vmem, anywhere] + [vmem] * len(known),
        out_specs=anywhere,
        scratch_shapes=[
            pltpu.VMEM((slots, width), jnp.bfloat16),
            pltpu.VMEM((count, width), dtype),
            pltpu.SemaphoreType.DMA((PIECES,)),
            pltpu.SemaphoreType.DMA((PIECES,)),
        ],
        compiler_params=pltpu.CompilerParams(vmem_limit_bytes=VMEM_BYTES),
        cost_estimate=pl.CostEstimate(
            flops=4 * count * slots * width, transcendentals=0, bytes_accessed=2 * slots * width
        ),
    )(table, rows, *known)


def exchange(rows, devices):
    count, width = rows.shape
    split = rows.reshape(devices, count // devices, width)
    return lax.all_to_all(split, "ep", split_axis=0, concat_axis=0, tiled=True).reshape(
        count, width
    )


def on_device(tokens, expert_ids, affinity, w_gate, w_up, w_down):
    devices = lax.axis_size("ep")
    experts = devices // 2
    slots = 2 * tokens.shape[0] * TOP // experts
    mates = [[s, s + 1] for s in range(0, devices, 2)]
    gates, ups, downs = [
        lax.all_gather(w, "ep", axis_index_groups=mates, axis=0, tiled=True)
        for w in (w_gate, w_up, w_down)
    ]
    turned_ids = expert_ids.T
    table = weights_of_slots(turned_ids, affinity.T, experts, slots, CHUNKS)
    parts = []
    for chunk in range(CHUNKS):
        rows = exchange(slots_of_tokens(tokens, turned_ids, experts, slots, chunk), devices)
        computed = down_rows(hidden_units(rows, gates, ups), downs)
        parts.append(exchange(computed, devices))
    known = []
    for chunk in range(CHUNKS - 1):
        known = [mix(table[chunk], parts[chunk], known, jnp.float32)]
    return mix(table[CHUNKS - 1], parts[CHUNKS - 1], known, jnp.bfloat16)


def solution(mesh):
    rows = P(("dp", "ep"), None)
    weights = P("ep", None, None)
    return jax.shard_map(
        on_device,
        mesh=mesh,
        in_specs=(rows, rows, rows, weights, weights, weights),
        out_specs=rows,
        check_vma=False,
    )
```

```python
import functools
import jax
import jax.numpy as jnp
from jax import lax
from jax.experimental import pallas as pl
from jax.experimental.pallas import tpu as pltpu
from jax.sharding import PartitionSpec as P

TOP = 2
BLOCK = 16
LANES = 128
CHUNKS = 2
PIECES = 7
VMEM_BYTES = 56 * 1024 * 1024


def iota(shape, dim):
    return lax.broadcasted_iota(jnp.int32, shape, dim)


def halves(value):
    upper = value.astype(jnp.bfloat16)
    return upper, (value - upper.astype(jnp.float32)).astype(jnp.bfloat16)


def ones_where(hit):
    return hit.astype(jnp.float32).astype(jnp.bfloat16)


def times(a, b):
    return jnp.dot(a, b, preferred_element_type=jnp.float32)


def slot_keys(turned_ids_ref, experts):
    count = turned_ids_ref.shape[1]
    row = iota((experts, count), 0)
    hit = turned_ids_ref[0:1, :] == row
    for k in range(1, TOP):
        hit = hit | (turned_ids_ref[k : k + 1, :] == row)
    earlier = ones_where(iota((count, count), 0) < iota((count, count), 1))
    rank = times(ones_where(hit), earlier)
    return jnp.where(hit, rank, -1.0).astype(jnp.bfloat16)


def restored_rows(tokens, gather, spread, spread3):
    x = tokens.astype(jnp.float32)
    width = x.shape[1]
    tops = []
    for at in range(0, width, LANES):
        top = jnp.abs(x[:, at : at + LANES])
        for step in (1, 2, 4, 8):
            top = jnp.maximum(top, pltpu.roll(top, LANES - step, 1))
        tops.append(top.astype(jnp.bfloat16))
    largest = times(jnp.concatenate(tops, axis=1), gather)
    scale = (jnp.maximum(largest, 0.25) / 9.0).astype(jnp.bfloat16)
    inverse = 1.0 / scale.astype(jnp.float32)
    first, rest = halves(inverse)
    second, third = halves(inverse - first.astype(jnp.float32))
    inverse = times(jnp.concatenate([first, second, third], axis=1), spread3)
    scale = times(scale, spread)
    payload = jnp.clip(x * inverse, -6.0, 6.0).astype(jnp.bfloat16).astype(jnp.float32)
    return (payload * scale).astype(jnp.bfloat16)


def pick_kernel(experts, chunk, ids_ref, tokens_ref, out_ref, tokens, rows_out, pick, got, put):
    count, width = tokens.shape
    rows = rows_out.shape[0]
    each = rows // experts
    pieces = got.shape[0]
    wide = width // pieces

    def loaded(i):
        part = (slice(None), pl.ds(i * wide, wide))
        return pltpu.make_async_copy(tokens_ref.at[part], tokens.at[part], got.at[i])

    def stored(i):
        part = (slice(None), pl.ds(i * wide, wide))
        return pltpu.make_async_copy(rows_out.at[part], out_ref.at[part], put.at[i])

    for i in range(pieces):
        loaded(i).start()
    key = slot_keys(ids_ref, experts)
    all_keys = times(ones_where(iota((rows, experts), 0) // each == iota((rows, experts), 1)), key)
    place = (iota((rows, count), 0) % each + each * chunk).astype(jnp.float32)
    pick[...] = ones_where(all_keys == place)
    for i in range(pieces):
        loaded(i).wait()
        part = tokens[:, i * wide : (i + 1) * wide]
        rows_out[:, i * wide : (i + 1) * wide] = times(pick[...], part).astype(jnp.bfloat16)
        stored(i).start()
    for i in range(pieces):
        stored(i).wait()


def slots_of_tokens(tokens, turned_ids, experts, slots, chunk):
    count, width = tokens.shape
    rows = experts * slots // CHUNKS
    return pl.pallas_call(
        functools.partial(pick_kernel, experts, chunk),
        name="pick_slots",
        out_shape=jax.ShapeDtypeStruct((rows, width), jnp.bfloat16),
        in_specs=[pl.BlockSpec(memory_space=pltpu.VMEM), pl.BlockSpec(memory_space=pl.ANY)],
        out_specs=pl.BlockSpec(memory_space=pl.ANY),
        scratch_shapes=[
            pltpu.VMEM((count, width), jnp.bfloat16),
            pltpu.VMEM((rows, width), jnp.bfloat16),
            pltpu.VMEM((rows, count), jnp.bfloat16),
            pltpu.SemaphoreType.DMA((PIECES,)),
            pltpu.SemaphoreType.DMA((PIECES,)),
        ],
        compiler_params=pltpu.CompilerParams(vmem_limit_bytes=VMEM_BYTES),
    )(turned_ids, tokens)


def expert_kernel(
    steps,
    x_ref,
    g0,
    g1,
    u0,
    u1,
    d0,
    d1,
    out_ref,
    gate0,
    gate1,
    up0,
    up1,
    hid0,
    hid1,
    gather,
    spread,
    spread3,
):
    step = pl.program_id(0)
    pairs = ((gate0, g0), (gate1, g1), (up0, u0), (up1, u1))

    @pl.when(step == 0)
    def _():
        for total, _w in pairs:
            total[...] = jnp.zeros_like(total)
        width, blocks = gather.shape
        gather[...] = ones_where(iota((width, blocks), 0) == BLOCK * iota((width, blocks), 1))
        spread[...] = ones_where(iota((blocks, width), 1) // BLOCK == iota((blocks, width), 0))
        for j in range(3):
            spread3[j * blocks : (j + 1) * blocks, :] = spread[...]

    @pl.when(step < steps)
    def _():
        x = restored_rows(x_ref[...], gather[...], spread[...], spread3[...])
        for total, w in pairs:
            total[...] += jnp.dot(x, w[...], preferred_element_type=jnp.float32)

    @pl.when(step == steps - 1)
    def _():
        for hid, gate, up in ((hid0, gate0, up0), (hid1, gate1, up1)):
            v = gate[...]
            hid[...] = (v / (1.0 + jnp.exp(-v)) * up[...]).astype(jnp.bfloat16)

    @pl.when(step >= steps)
    def _():
        out_ref[...] = (
            jnp.dot(hid0[...], d0[...], preferred_element_type=jnp.float32)
            + jnp.dot(hid1[...], d1[...], preferred_element_type=jnp.float32)
        ).astype(jnp.bfloat16)


def expert(rows, gates, ups, downs):
    count, width = rows.shape
    half = gates[0].shape[-1]
    wide = 1024
    steps = width // wide
    first = lambda s: jnp.minimum(s, steps - 1)
    second = lambda s: jnp.maximum(s - steps, 0)
    into = pl.BlockSpec((None, wide, half), lambda s: (0, first(s), 0))
    out_of = pl.BlockSpec((None, half, wide), lambda s: (0, 0, second(s)))
    return pl.pallas_call(
        functools.partial(expert_kernel, steps),
        name="expert_rows",
        out_shape=jax.ShapeDtypeStruct((count, width), jnp.bfloat16),
        grid=(2 * steps,),
        in_specs=[pl.BlockSpec((count, wide), lambda s: (0, first(s)))] + [into] * 4 + [out_of] * 2,
        out_specs=pl.BlockSpec((count, wide), lambda s: (0, second(s))),
        scratch_shapes=[pltpu.VMEM((count, half), jnp.float32)] * 4
        + [pltpu.VMEM((count, half), jnp.bfloat16)] * 2
        + [
            pltpu.VMEM((wide, wide // BLOCK), jnp.bfloat16),
            pltpu.VMEM((wide // BLOCK, wide), jnp.bfloat16),
            pltpu.VMEM((3 * wide // BLOCK, wide), jnp.bfloat16),
        ],
        compiler_params=pltpu.CompilerParams(
            dimension_semantics=("arbitrary",), vmem_limit_bytes=VMEM_BYTES
        ),
        cost_estimate=pl.CostEstimate(
            flops=count * width * half * 12,
            transcendentals=count * half * 2,
            bytes_accessed=width * half * 12 + count * width * 4,
        ),
    )(rows, *gates, *ups, *downs)


def table_kernel(experts, chunks, ids_ref, affinity_ref, *out_refs):
    count = ids_ref.shape[1]
    rows = out_refs[0].shape[1]
    each = rows // experts
    key = slot_keys(ids_ref, experts)
    total = affinity_ref[0:1, :]
    for k in range(1, TOP):
        total = total + affinity_ref[k : k + 1, :]
    row = iota((experts, count), 0)
    weight = jnp.zeros((experts, count), jnp.float32)
    for k in range(TOP):
        share = affinity_ref[k : k + 1, :] / total
        weight = jnp.where(ids_ref[k : k + 1, :] == row, share, weight)
    same = ones_where(iota((count, count), 0) == iota((count, count), 1))
    spread = ones_where(iota((experts, rows), 1) // each == iota((experts, rows), 0))

    def by_token(value):
        turned = lax.dot_general(
            same, value, (((1,), (1,)), ((), ())), preferred_element_type=jnp.float32
        )
        return times(turned.astype(jnp.bfloat16), spread)

    wide = by_token(key)
    upper, lower = [by_token(part) for part in halves(weight)]
    place = (iota((count, rows), 1) % each).astype(jnp.float32)
    for j in range(chunks):
        hit = wide == place + float(each * j)
        out_refs[j][0:count, :] = jnp.where(hit, upper, 0.0).astype(jnp.bfloat16)
        out_refs[j][count : 2 * count, :] = jnp.where(hit, lower, 0.0).astype(jnp.bfloat16)


def weights_of_slots(turned_ids, turned_affinity, experts, slots, chunks):
    count = turned_ids.shape[1]
    rows = experts * slots // chunks
    return pl.pallas_call(
        functools.partial(table_kernel, experts, chunks),
        name="slot_weights",
        out_shape=[jax.ShapeDtypeStruct((2 * count, rows), jnp.bfloat16)] * chunks,
    )(turned_ids, turned_affinity)


def mix_kernel(table_ref, in_ref, *rest):
    known_refs, out_ref = rest[:-5], rest[-5]
    values, mixed, got, put = rest[-4:]
    count, width = mixed.shape
    pieces = put.shape[0]
    wide = width // pieces

    def part(i):
        return (slice(None), pl.ds(i * wide, wide))

    def loaded(i):
        return pltpu.make_async_copy(in_ref.at[part(i)], values.at[part(i)], got.at[i])

    def stored(i):
        return pltpu.make_async_copy(mixed.at[part(i)], out_ref.at[part(i)], put.at[i])

    for i in range(pieces):
        loaded(i).start()
    for i in range(pieces):
        loaded(i).wait()
        both = times(table_ref[...], values[:, i * wide : (i + 1) * wide])
        total = both[:count] + both[count:]
        for known in known_refs:
            total = total + known[:, i * wide : (i + 1) * wide]
        mixed[:, i * wide : (i + 1) * wide] = total.astype(mixed.dtype)
        stored(i).start()
    for i in range(pieces):
        stored(i).wait()


def mix(table, rows, known, dtype):
    count = table.shape[0] // 2
    slots, width = rows.shape
    anywhere = pl.BlockSpec(memory_space=pl.ANY)
    vmem = pl.BlockSpec(memory_space=pltpu.VMEM)
    return pl.pallas_call(
        mix_kernel,
        name="mix_slots",
        out_shape=jax.ShapeDtypeStruct((count, width), dtype),
        in_specs=[vmem, anywhere] + [vmem] * len(known),
        out_specs=anywhere,
        scratch_shapes=[
            pltpu.VMEM((slots, width), jnp.bfloat16),
            pltpu.VMEM((count, width), dtype),
            pltpu.SemaphoreType.DMA((PIECES,)),
            pltpu.SemaphoreType.DMA((PIECES,)),
        ],
        compiler_params=pltpu.CompilerParams(vmem_limit_bytes=VMEM_BYTES),
        cost_estimate=pl.CostEstimate(
            flops=4 * count * slots * width, transcendentals=0, bytes_accessed=2 * slots * width
        ),
    )(table, rows, *known)


def exchange(rows, devices):
    count, width = rows.shape
    split = rows.reshape(devices, count // devices, width)
    return lax.all_to_all(split, "ep", split_axis=0, concat_axis=0, tiled=True).reshape(
        count, width
    )


def on_device(tokens, expert_ids, affinity, w_gate, w_up, w_down):
    devices = lax.axis_size("ep")
    experts = devices // 2
    slots = 2 * tokens.shape[0] * TOP // experts
    pairs = [(s, s ^ 1) for s in range(devices)]
    gates, ups, downs = [(w, lax.ppermute(w, "ep", pairs)) for w in (w_gate, w_up, w_down)]
    turned_ids = expert_ids.T
    table = weights_of_slots(turned_ids, affinity.T, experts, slots, CHUNKS)
    parts = []
    for chunk in range(CHUNKS):
        rows = exchange(slots_of_tokens(tokens, turned_ids, experts, slots, chunk), devices)
        parts.append(exchange(expert(rows, gates, ups, downs), devices))
    known = []
    for chunk in range(CHUNKS - 1):
        known = [mix(table[chunk], parts[chunk], known, jnp.float32)]
    return mix(table[CHUNKS - 1], parts[CHUNKS - 1], known, jnp.bfloat16)


def solution(mesh):
    rows = P(("dp", "ep"), None)
    weights = P("ep", None, None)
    return jax.shard_map(
        on_device,
        mesh=mesh,
        in_specs=(rows, rows, rows, weights, weights, weights),
        out_specs=rows,
        check_vma=False,
    )
```

```python
import functools
import jax
import jax.numpy as jnp
from jax import lax
from jax.experimental import pallas as pl
from jax.experimental.pallas import tpu as pltpu
from jax.sharding import PartitionSpec as P

TOP = 2
BLOCK = 16
LANES = 128
CHUNKS = 2
PIECES = 7
VMEM_BYTES = 56 * 1024 * 1024


def iota(shape, dim):
    return lax.broadcasted_iota(jnp.int32, shape, dim)


def halves(value):
    upper = value.astype(jnp.bfloat16)
    return upper, (value - upper.astype(jnp.float32)).astype(jnp.bfloat16)


def ones_where(hit):
    return hit.astype(jnp.float32).astype(jnp.bfloat16)


def times(a, b):
    return jnp.dot(a, b, preferred_element_type=jnp.float32)


def slot_keys(turned_ids_ref, experts):
    count = turned_ids_ref.shape[1]
    row = iota((experts, count), 0)
    hit = turned_ids_ref[0:1, :] == row
    for k in range(1, TOP):
        hit = hit | (turned_ids_ref[k : k + 1, :] == row)
    earlier = ones_where(iota((count, count), 0) < iota((count, count), 1))
    rank = times(ones_where(hit), earlier)
    return jnp.where(hit, rank, -1.0).astype(jnp.bfloat16)


def restored_rows(tokens, gather, spread, spread3):
    x = tokens.astype(jnp.float32)
    width = x.shape[1]
    tops = []
    for at in range(0, width, LANES):
        top = jnp.abs(x[:, at : at + LANES])
        for step in (1, 2, 4, 8):
            top = jnp.maximum(top, pltpu.roll(top, LANES - step, 1))
        tops.append(top.astype(jnp.bfloat16))
    largest = times(jnp.concatenate(tops, axis=1), gather)
    scale = (jnp.maximum(largest, 0.25) / 9.0).astype(jnp.bfloat16)
    inverse = 1.0 / scale.astype(jnp.float32)
    first, rest = halves(inverse)
    second, third = halves(inverse - first.astype(jnp.float32))
    inverse = times(jnp.concatenate([first, second, third], axis=1), spread3)
    scale = times(scale, spread)
    payload = jnp.clip(x * inverse, -6.0, 6.0).astype(jnp.bfloat16).astype(jnp.float32)
    return (payload * scale).astype(jnp.bfloat16)


def pick_kernel(experts, chunk, ids_ref, tokens_ref, out_ref, tokens, rows_out, pick, got, put):
    count, width = tokens.shape
    rows = rows_out.shape[0]
    each = rows // experts
    pieces = got.shape[0]
    wide = width // pieces

    def loaded(i):
        part = (slice(None), pl.ds(i * wide, wide))
        return pltpu.make_async_copy(tokens_ref.at[part], tokens.at[part], got.at[i])

    def stored(i):
        part = (slice(None), pl.ds(i * wide, wide))
        return pltpu.make_async_copy(rows_out.at[part], out_ref.at[part], put.at[i])

    for i in range(pieces):
        loaded(i).start()
    key = slot_keys(ids_ref, experts)
    all_keys = times(ones_where(iota((rows, experts), 0) // each == iota((rows, experts), 1)), key)
    place = (iota((rows, count), 0) % each + each * chunk).astype(jnp.float32)
    pick[...] = ones_where(all_keys == place)
    for i in range(pieces):
        loaded(i).wait()
        part = tokens[:, i * wide : (i + 1) * wide]
        rows_out[:, i * wide : (i + 1) * wide] = times(pick[...], part).astype(jnp.bfloat16)
        stored(i).start()
    for i in range(pieces):
        stored(i).wait()


def slots_of_tokens(tokens, turned_ids, experts, slots, chunk):
    count, width = tokens.shape
    rows = experts * slots // CHUNKS
    return pl.pallas_call(
        functools.partial(pick_kernel, experts, chunk),
        name="pick_slots",
        out_shape=jax.ShapeDtypeStruct((rows, width), jnp.bfloat16),
        in_specs=[pl.BlockSpec(memory_space=pltpu.VMEM), pl.BlockSpec(memory_space=pl.ANY)],
        out_specs=pl.BlockSpec(memory_space=pl.ANY),
        scratch_shapes=[
            pltpu.VMEM((count, width), jnp.bfloat16),
            pltpu.VMEM((rows, width), jnp.bfloat16),
            pltpu.VMEM((rows, count), jnp.bfloat16),
            pltpu.SemaphoreType.DMA((PIECES,)),
            pltpu.SemaphoreType.DMA((PIECES,)),
        ],
        compiler_params=pltpu.CompilerParams(vmem_limit_bytes=VMEM_BYTES),
    )(turned_ids, tokens)


def expert_kernel(
    steps,
    x_ref,
    g0,
    g1,
    u0,
    u1,
    d0,
    d1,
    out_ref,
    gate0,
    gate1,
    up0,
    up1,
    hid0,
    hid1,
    gather,
    spread,
    spread3,
):
    step = pl.program_id(0)
    pairs = ((gate0, g0), (gate1, g1), (up0, u0), (up1, u1))

    @pl.when(step == 0)
    def _():
        for total, _w in pairs:
            total[...] = jnp.zeros_like(total)
        width, blocks = gather.shape
        gather[...] = ones_where(iota((width, blocks), 0) == BLOCK * iota((width, blocks), 1))
        spread[...] = ones_where(iota((blocks, width), 1) // BLOCK == iota((blocks, width), 0))
        for j in range(3):
            spread3[j * blocks : (j + 1) * blocks, :] = spread[...]

    @pl.when(step < steps)
    def _():
        x = restored_rows(x_ref[...], gather[...], spread[...], spread3[...])
        for total, w in pairs:
            total[...] += jnp.dot(x, w[...], preferred_element_type=jnp.float32)

    @pl.when(step == steps - 1)
    def _():
        for hid, gate, up in ((hid0, gate0, up0), (hid1, gate1, up1)):
            v = gate[...]
            hid[...] = (v / (1.0 + jnp.exp(-v)) * up[...]).astype(jnp.bfloat16)

    @pl.when(step >= steps)
    def _():
        out_ref[...] = (
            jnp.dot(hid0[...], d0[...], preferred_element_type=jnp.float32)
            + jnp.dot(hid1[...], d1[...], preferred_element_type=jnp.float32)
        ).astype(jnp.bfloat16)


def expert(rows, gates, ups, downs):
    count, width = rows.shape
    half = gates[0].shape[-1]
    wide = 1024
    steps = width // wide
    first = lambda s: jnp.minimum(s, steps - 1)
    second = lambda s: jnp.maximum(s - steps, 0)
    into = pl.BlockSpec((None, wide, half), lambda s: (0, first(s), 0))
    out_of = pl.BlockSpec((None, half, wide), lambda s: (0, 0, second(s)))
    return pl.pallas_call(
        functools.partial(expert_kernel, steps),
        name="expert_rows",
        out_shape=jax.ShapeDtypeStruct((count, width), jnp.bfloat16),
        grid=(2 * steps,),
        in_specs=[pl.BlockSpec((count, wide), lambda s: (0, first(s)))] + [into] * 4 + [out_of] * 2,
        out_specs=pl.BlockSpec((count, wide), lambda s: (0, second(s))),
        scratch_shapes=[pltpu.VMEM((count, half), jnp.float32)] * 4
        + [pltpu.VMEM((count, half), jnp.bfloat16)] * 2
        + [
            pltpu.VMEM((wide, wide // BLOCK), jnp.bfloat16),
            pltpu.VMEM((wide // BLOCK, wide), jnp.bfloat16),
            pltpu.VMEM((3 * wide // BLOCK, wide), jnp.bfloat16),
        ],
        compiler_params=pltpu.CompilerParams(
            dimension_semantics=("arbitrary",), vmem_limit_bytes=VMEM_BYTES
        ),
        cost_estimate=pl.CostEstimate(
            flops=count * width * half * 12,
            transcendentals=count * half * 2,
            bytes_accessed=width * half * 12 + count * width * 4,
        ),
    )(rows, *gates, *ups, *downs)


def table_kernel(experts, chunks, ids_ref, affinity_ref, *out_refs):
    count = ids_ref.shape[1]
    rows = out_refs[0].shape[1]
    each = rows // experts
    key = slot_keys(ids_ref, experts)
    total = affinity_ref[0:1, :]
    for k in range(1, TOP):
        total = total + affinity_ref[k : k + 1, :]
    row = iota((experts, count), 0)
    weight = jnp.zeros((experts, count), jnp.float32)
    for k in range(TOP):
        share = affinity_ref[k : k + 1, :] / total
        weight = jnp.where(ids_ref[k : k + 1, :] == row, share, weight)
    same = ones_where(iota((count, count), 0) == iota((count, count), 1))
    spread = ones_where(iota((experts, rows), 1) // each == iota((experts, rows), 0))

    def by_token(value):
        turned = lax.dot_general(
            same, value, (((1,), (1,)), ((), ())), preferred_element_type=jnp.float32
        )
        return times(turned.astype(jnp.bfloat16), spread)

    wide = by_token(key)
    upper, lower = [by_token(part) for part in halves(weight)]
    place = (iota((count, rows), 1) % each).astype(jnp.float32)
    for j in range(chunks):
        hit = wide == place + float(each * j)
        out_refs[j][0:count, :] = jnp.where(hit, upper, 0.0).astype(jnp.bfloat16)
        out_refs[j][count : 2 * count, :] = jnp.where(hit, lower, 0.0).astype(jnp.bfloat16)


def weights_of_slots(turned_ids, turned_affinity, experts, slots, chunks):
    count = turned_ids.shape[1]
    rows = experts * slots // chunks
    return pl.pallas_call(
        functools.partial(table_kernel, experts, chunks),
        name="slot_weights",
        out_shape=[jax.ShapeDtypeStruct((2 * count, rows), jnp.bfloat16)] * chunks,
    )(turned_ids, turned_affinity)


def mix_kernel(table_ref, in_ref, *rest):
    known_refs, out_ref = rest[:-7], rest[-7]
    values, mixed, known, got, put, held = rest[-6:]
    count, width = mixed.shape
    pieces = put.shape[0]
    wide = width // pieces

    def part(i):
        return (slice(None), pl.ds(i * wide, wide))

    def loaded(i):
        return pltpu.make_async_copy(in_ref.at[part(i)], values.at[part(i)], got.at[i])

    def stored(i):
        return pltpu.make_async_copy(mixed.at[part(i)], out_ref.at[part(i)], put.at[i])

    def kept(i):
        return pltpu.make_async_copy(known_refs[0].at[part(i)], known.at[part(i)], held.at[i])

    for i in range(pieces):
        loaded(i).start()
        if known_refs:
            kept(i).start()
    for i in range(pieces):
        loaded(i).wait()
        both = times(table_ref[...], values[:, i * wide : (i + 1) * wide])
        total = both[:count] + both[count:]
        if known_refs:
            kept(i).wait()
            total = total + known[:, i * wide : (i + 1) * wide].astype(jnp.float32)
        mixed[:, i * wide : (i + 1) * wide] = total.astype(mixed.dtype)
        stored(i).start()
    for i in range(pieces):
        stored(i).wait()


def mix(table, rows, known):
    count = table.shape[0] // 2
    slots, width = rows.shape
    anywhere = pl.BlockSpec(memory_space=pl.ANY)
    vmem = pl.BlockSpec(memory_space=pltpu.VMEM)
    return pl.pallas_call(
        mix_kernel,
        name="mix_slots",
        out_shape=jax.ShapeDtypeStruct((count, width), jnp.bfloat16),
        in_specs=[vmem, anywhere] + [anywhere] * len(known),
        out_specs=anywhere,
        scratch_shapes=[
            pltpu.VMEM((slots, width), jnp.bfloat16),
            pltpu.VMEM((count, width), jnp.bfloat16),
            pltpu.VMEM((count, width), jnp.bfloat16),
            pltpu.SemaphoreType.DMA((PIECES,)),
            pltpu.SemaphoreType.DMA((PIECES,)),
            pltpu.SemaphoreType.DMA((PIECES,)),
        ],
        compiler_params=pltpu.CompilerParams(vmem_limit_bytes=VMEM_BYTES),
        cost_estimate=pl.CostEstimate(
            flops=4 * count * slots * width, transcendentals=0, bytes_accessed=2 * slots * width
        ),
    )(table, rows, *known)


def exchange(rows, devices):
    count, width = rows.shape
    split = rows.reshape(devices, count // devices, width)
    return lax.all_to_all(split, "ep", split_axis=0, concat_axis=0, tiled=True).reshape(
        count, width
    )


def on_device(tokens, expert_ids, affinity, w_gate, w_up, w_down):
    devices = lax.axis_size("ep")
    experts = devices // 2
    slots = 2 * tokens.shape[0] * TOP // experts
    pairs = [(s, s ^ 1) for s in range(devices)]
    gates, ups, downs = [(w, lax.ppermute(w, "ep", pairs)) for w in (w_gate, w_up, w_down)]
    turned_ids = expert_ids.T
    table = weights_of_slots(turned_ids, affinity.T, experts, slots, CHUNKS)
    parts = []
    for chunk in range(CHUNKS):
        rows = exchange(slots_of_tokens(tokens, turned_ids, experts, slots, chunk), devices)
        parts.append(exchange(expert(rows, gates, ups, downs), devices))
    known = []
    for chunk in range(CHUNKS - 1):
        known = [mix(table[chunk], parts[chunk], known)]
    return mix(table[CHUNKS - 1], parts[CHUNKS - 1], known)


def solution(mesh):
    rows = P(("dp", "ep"), None)
    weights = P("ep", None, None)
    return jax.shard_map(
        on_device,
        mesh=mesh,
        in_specs=(rows, rows, rows, weights, weights, weights),
        out_specs=rows,
        check_vma=False,
    )
```

```python
import functools
import jax
import jax.numpy as jnp
from jax import lax
from jax.experimental import pallas as pl
from jax.experimental.pallas import tpu as pltpu
from jax.sharding import PartitionSpec as P

TOP = 2
BLOCK = 16
LANES = 128
CHUNKS = 2
PIECES = 7
VMEM_BYTES = 56 * 1024 * 1024


def iota(shape, dim):
    return lax.broadcasted_iota(jnp.int32, shape, dim)


def halves(value):
    upper = value.astype(jnp.bfloat16)
    return upper, (value - upper.astype(jnp.float32)).astype(jnp.bfloat16)


def ones_where(hit):
    return hit.astype(jnp.float32).astype(jnp.bfloat16)


def times(a, b):
    return jnp.dot(a, b, preferred_element_type=jnp.float32)


def slot_keys(turned_ids_ref, experts):
    count = turned_ids_ref.shape[1]
    row = iota((experts, count), 0)
    hit = turned_ids_ref[0:1, :] == row
    for k in range(1, TOP):
        hit = hit | (turned_ids_ref[k : k + 1, :] == row)
    earlier = ones_where(iota((count, count), 0) < iota((count, count), 1))
    rank = times(ones_where(hit), earlier)
    return jnp.where(hit, rank, -1.0).astype(jnp.bfloat16)


def restored_rows(tokens, gather, spread, spread3):
    x = tokens.astype(jnp.float32)
    width = x.shape[1]
    tops = []
    for at in range(0, width, LANES):
        top = jnp.abs(x[:, at : at + LANES])
        for step in (1, 2, 4, 8):
            top = jnp.maximum(top, pltpu.roll(top, LANES - step, 1))
        tops.append(top.astype(jnp.bfloat16))
    largest = times(jnp.concatenate(tops, axis=1), gather)
    scale = (jnp.maximum(largest, 0.25) / 9.0).astype(jnp.bfloat16)
    inverse = 1.0 / scale.astype(jnp.float32)
    first, rest = halves(inverse)
    second, third = halves(inverse - first.astype(jnp.float32))
    inverse = times(jnp.concatenate([first, second, third], axis=1), spread3)
    scale = times(scale, spread)
    payload = jnp.clip(x * inverse, -6.0, 6.0).astype(jnp.bfloat16).astype(jnp.float32)
    return (payload * scale).astype(jnp.bfloat16)


def pick_kernel(
    experts, chunk, ids_in, tokens_ref, out_ref, ids_ref, tokens, rows_out, pick, got, put, first
):
    count, width = tokens.shape
    rows = rows_out.shape[0]
    each = rows // experts
    pieces = got.shape[0]
    wide = width // pieces

    def loaded(i):
        part = (slice(None), pl.ds(i * wide, wide))
        return pltpu.make_async_copy(tokens_ref.at[part], tokens.at[part], got.at[i])

    def stored(i):
        part = (slice(None), pl.ds(i * wide, wide))
        return pltpu.make_async_copy(rows_out.at[part], out_ref.at[part], put.at[i])

    ids_copy = pltpu.make_async_copy(ids_in, ids_ref, first)
    ids_copy.start()
    for i in range(pieces):
        loaded(i).start()
    ids_copy.wait()
    key = slot_keys(ids_ref, experts)
    all_keys = times(ones_where(iota((rows, experts), 0) // each == iota((rows, experts), 1)), key)
    place = (iota((rows, count), 0) % each + each * chunk).astype(jnp.float32)
    pick[...] = ones_where(all_keys == place)
    for i in range(pieces):
        loaded(i).wait()
        part = tokens[:, i * wide : (i + 1) * wide]
        rows_out[:, i * wide : (i + 1) * wide] = times(pick[...], part).astype(jnp.bfloat16)
        stored(i).start()
    for i in range(pieces):
        stored(i).wait()


def slots_of_tokens(tokens, turned_ids, experts, slots, chunk):
    count, width = tokens.shape
    rows = experts * slots // CHUNKS
    return pl.pallas_call(
        functools.partial(pick_kernel, experts, chunk),
        name="pick_slots",
        out_shape=jax.ShapeDtypeStruct((rows, width), jnp.bfloat16),
        in_specs=[pl.BlockSpec(memory_space=pl.ANY)] * 2,
        out_specs=pl.BlockSpec(memory_space=pl.ANY),
        scratch_shapes=[
            pltpu.VMEM((TOP, count), jnp.int32),
            pltpu.VMEM((count, width), jnp.bfloat16),
            pltpu.VMEM((rows, width), jnp.bfloat16),
            pltpu.VMEM((rows, count), jnp.bfloat16),
            pltpu.SemaphoreType.DMA((PIECES,)),
            pltpu.SemaphoreType.DMA((PIECES,)),
            pltpu.SemaphoreType.DMA,
        ],
        compiler_params=pltpu.CompilerParams(vmem_limit_bytes=VMEM_BYTES),
    )(turned_ids, tokens)


def expert_kernel(
    steps,
    x_ref,
    g0,
    g1,
    u0,
    u1,
    d0,
    d1,
    out_ref,
    gate0,
    gate1,
    up0,
    up1,
    hid0,
    hid1,
    gather,
    spread,
    spread3,
):
    step = pl.program_id(0)
    pairs = ((gate0, g0), (gate1, g1), (up0, u0), (up1, u1))

    @pl.when(step == 0)
    def _():
        for total, _w in pairs:
            total[...] = jnp.zeros_like(total)
        width, blocks = gather.shape
        gather[...] = ones_where(iota((width, blocks), 0) == BLOCK * iota((width, blocks), 1))
        spread[...] = ones_where(iota((blocks, width), 1) // BLOCK == iota((blocks, width), 0))
        for j in range(3):
            spread3[j * blocks : (j + 1) * blocks, :] = spread[...]

    @pl.when(step < steps)
    def _():
        x = restored_rows(x_ref[...], gather[...], spread[...], spread3[...])
        for total, w in pairs:
            total[...] += jnp.dot(x, w[...], preferred_element_type=jnp.float32)

    @pl.when(step == steps - 1)
    def _():
        for hid, gate, up in ((hid0, gate0, up0), (hid1, gate1, up1)):
            v = gate[...]
            hid[...] = (v / (1.0 + jnp.exp(-v)) * up[...]).astype(jnp.bfloat16)

    @pl.when(step >= steps)
    def _():
        out_ref[...] = (
            jnp.dot(hid0[...], d0[...], preferred_element_type=jnp.float32)
            + jnp.dot(hid1[...], d1[...], preferred_element_type=jnp.float32)
        ).astype(jnp.bfloat16)


def expert(rows, gates, ups, downs):
    count, width = rows.shape
    half = gates[0].shape[-1]
    wide = 1024
    steps = width // wide
    first = lambda s: jnp.minimum(s, steps - 1)
    second = lambda s: jnp.maximum(s - steps, 0)
    into = pl.BlockSpec((None, wide, half), lambda s: (0, first(s), 0))
    out_of = pl.BlockSpec((None, half, wide), lambda s: (0, 0, second(s)))
    return pl.pallas_call(
        functools.partial(expert_kernel, steps),
        name="expert_rows",
        out_shape=jax.ShapeDtypeStruct((count, width), jnp.bfloat16),
        grid=(2 * steps,),
        in_specs=[pl.BlockSpec((count, wide), lambda s: (0, first(s)))] + [into] * 4 + [out_of] * 2,
        out_specs=pl.BlockSpec((count, wide), lambda s: (0, second(s))),
        scratch_shapes=[pltpu.VMEM((count, half), jnp.float32)] * 4
        + [pltpu.VMEM((count, half), jnp.bfloat16)] * 2
        + [
            pltpu.VMEM((wide, wide // BLOCK), jnp.bfloat16),
            pltpu.VMEM((wide // BLOCK, wide), jnp.bfloat16),
            pltpu.VMEM((3 * wide // BLOCK, wide), jnp.bfloat16),
        ],
        compiler_params=pltpu.CompilerParams(
            dimension_semantics=("arbitrary",), vmem_limit_bytes=VMEM_BYTES
        ),
        cost_estimate=pl.CostEstimate(
            flops=count * width * half * 12,
            transcendentals=count * half * 2,
            bytes_accessed=width * half * 12 + count * width * 4,
        ),
    )(rows, *gates, *ups, *downs)


def table_kernel(experts, chunks, ids_ref, affinity_ref, *out_refs):
    count = ids_ref.shape[1]
    rows = out_refs[0].shape[1]
    each = rows // experts
    key = slot_keys(ids_ref, experts)
    total = affinity_ref[0:1, :]
    for k in range(1, TOP):
        total = total + affinity_ref[k : k + 1, :]
    row = iota((experts, count), 0)
    weight = jnp.zeros((experts, count), jnp.float32)
    for k in range(TOP):
        share = affinity_ref[k : k + 1, :] / total
        weight = jnp.where(ids_ref[k : k + 1, :] == row, share, weight)
    same = ones_where(iota((count, count), 0) == iota((count, count), 1))
    spread = ones_where(iota((experts, rows), 1) // each == iota((experts, rows), 0))

    def by_token(value):
        turned = lax.dot_general(
            same, value, (((1,), (1,)), ((), ())), preferred_element_type=jnp.float32
        )
        return times(turned.astype(jnp.bfloat16), spread)

    wide = by_token(key)
    upper, lower = [by_token(part) for part in halves(weight)]
    place = (iota((count, rows), 1) % each).astype(jnp.float32)
    for j in range(chunks):
        hit = wide == place + float(each * j)
        out_refs[j][0:count, :] = jnp.where(hit, upper, 0.0).astype(jnp.bfloat16)
        out_refs[j][count : 2 * count, :] = jnp.where(hit, lower, 0.0).astype(jnp.bfloat16)


def weights_of_slots(turned_ids, turned_affinity, experts, slots, chunks):
    count = turned_ids.shape[1]
    rows = experts * slots // chunks
    return pl.pallas_call(
        functools.partial(table_kernel, experts, chunks),
        name="slot_weights",
        out_shape=[jax.ShapeDtypeStruct((2 * count, rows), jnp.bfloat16)] * chunks,
    )(turned_ids, turned_affinity)


def mix_kernel(table_in, in_ref, *rest):
    known_refs, out_ref = rest[:-9], rest[-9]
    table_ref, values, mixed, known, got, put, held, first = rest[-8:]
    count, width = mixed.shape
    pieces = put.shape[0]
    wide = width // pieces

    def part(i):
        return (slice(None), pl.ds(i * wide, wide))

    def loaded(i):
        return pltpu.make_async_copy(in_ref.at[part(i)], values.at[part(i)], got.at[i])

    def stored(i):
        return pltpu.make_async_copy(mixed.at[part(i)], out_ref.at[part(i)], put.at[i])

    def kept(i):
        return pltpu.make_async_copy(known_refs[0].at[part(i)], known.at[part(i)], held.at[i])

    table_copy = pltpu.make_async_copy(table_in, table_ref, first)
    table_copy.start()
    for i in range(pieces):
        loaded(i).start()
        if known_refs:
            kept(i).start()
    table_copy.wait()
    for i in range(pieces):
        loaded(i).wait()
        both = times(table_ref[...], values[:, i * wide : (i + 1) * wide])
        total = both[:count] + both[count:]
        if known_refs:
            kept(i).wait()
            total = total + known[:, i * wide : (i + 1) * wide].astype(jnp.float32)
        mixed[:, i * wide : (i + 1) * wide] = total.astype(mixed.dtype)
        stored(i).start()
    for i in range(pieces):
        stored(i).wait()


def mix(table, rows, known):
    count = table.shape[0] // 2
    slots, width = rows.shape
    anywhere = pl.BlockSpec(memory_space=pl.ANY)
    return pl.pallas_call(
        mix_kernel,
        name="mix_slots",
        out_shape=jax.ShapeDtypeStruct((count, width), jnp.bfloat16),
        in_specs=[anywhere] * (2 + len(known)),
        out_specs=anywhere,
        scratch_shapes=[
            pltpu.VMEM(table.shape, jnp.bfloat16),
            pltpu.VMEM((slots, width), jnp.bfloat16),
            pltpu.VMEM((count, width), jnp.bfloat16),
            pltpu.VMEM((count, width), jnp.bfloat16),
            pltpu.SemaphoreType.DMA((PIECES,)),
            pltpu.SemaphoreType.DMA((PIECES,)),
            pltpu.SemaphoreType.DMA((PIECES,)),
            pltpu.SemaphoreType.DMA,
        ],
        compiler_params=pltpu.CompilerParams(vmem_limit_bytes=VMEM_BYTES),
        cost_estimate=pl.CostEstimate(
            flops=4 * count * slots * width, transcendentals=0, bytes_accessed=2 * slots * width
        ),
    )(table, rows, *known)


def exchange(rows, devices):
    count, width = rows.shape
    split = rows.reshape(devices, count // devices, width)
    return lax.all_to_all(split, "ep", split_axis=0, concat_axis=0, tiled=True).reshape(
        count, width
    )


def on_device(tokens, expert_ids, affinity, w_gate, w_up, w_down):
    devices = lax.axis_size("ep")
    experts = devices // 2
    slots = 2 * tokens.shape[0] * TOP // experts
    pairs = [(s, s ^ 1) for s in range(devices)]
    gates, ups, downs = [(w, lax.ppermute(w, "ep", pairs)) for w in (w_gate, w_up, w_down)]
    turned_ids = expert_ids.T
    table = weights_of_slots(turned_ids, affinity.T, experts, slots, CHUNKS)
    parts = []
    for chunk in range(CHUNKS):
        rows = exchange(slots_of_tokens(tokens, turned_ids, experts, slots, chunk), devices)
        parts.append(exchange(expert(rows, gates, ups, downs), devices))
    known = []
    for chunk in range(CHUNKS - 1):
        known = [mix(table[chunk], parts[chunk], known)]
    return mix(table[CHUNKS - 1], parts[CHUNKS - 1], known)


def solution(mesh):
    rows = P(("dp", "ep"), None)
    weights = P("ep", None, None)
    return jax.shard_map(
        on_device,
        mesh=mesh,
        in_specs=(rows, rows, rows, weights, weights, weights),
        out_specs=rows,
        check_vma=False,
    )
```

```python
import functools
import jax
import jax.numpy as jnp
from jax import lax
from jax.experimental import pallas as pl
from jax.experimental.pallas import tpu as pltpu
from jax.sharding import PartitionSpec as P

TOP = 2
BLOCK = 16
LANES = 128
CHUNKS = 2
PIECES = 7
VMEM_BYTES = 56 * 1024 * 1024


def iota(shape, dim):
    return lax.broadcasted_iota(jnp.int32, shape, dim)


def halves(value):
    upper = value.astype(jnp.bfloat16)
    return upper, (value - upper.astype(jnp.float32)).astype(jnp.bfloat16)


def ones_where(hit):
    return hit.astype(jnp.float32).astype(jnp.bfloat16)


def times(a, b):
    return jnp.dot(a, b, preferred_element_type=jnp.float32)


def slot_keys(turned_ids_ref, experts):
    count = turned_ids_ref.shape[1]
    row = iota((experts, count), 0)
    hit = turned_ids_ref[0:1, :] == row
    for k in range(1, TOP):
        hit = hit | (turned_ids_ref[k : k + 1, :] == row)
    earlier = ones_where(iota((count, count), 0) < iota((count, count), 1))
    rank = times(ones_where(hit), earlier)
    return jnp.where(hit, rank, -1.0).astype(jnp.bfloat16)


def restored_rows(tokens, gather, spread, spread3):
    x = tokens.astype(jnp.float32)
    width = x.shape[1]
    tops = []
    for at in range(0, width, LANES):
        top = jnp.abs(x[:, at : at + LANES])
        for step in (1, 2, 4, 8):
            top = jnp.maximum(top, pltpu.roll(top, LANES - step, 1))
        tops.append(top.astype(jnp.bfloat16))
    largest = times(jnp.concatenate(tops, axis=1), gather)
    scale = (jnp.maximum(largest, 0.25) / 9.0).astype(jnp.bfloat16)
    inverse = 1.0 / scale.astype(jnp.float32)
    first, rest = halves(inverse)
    second, third = halves(inverse - first.astype(jnp.float32))
    inverse = times(jnp.concatenate([first, second, third], axis=1), spread3)
    scale = times(scale, spread)
    payload = jnp.clip(x * inverse, -6.0, 6.0).astype(jnp.bfloat16).astype(jnp.float32)
    return (payload * scale).astype(jnp.bfloat16)


def pick_kernel(
    experts, chunk, ids_in, tokens_ref, out_ref, ids_ref, tokens, rows_out, pick, got, put, first
):
    count, width = tokens.shape
    rows = rows_out.shape[0]
    each = rows // experts
    pieces = got.shape[0]
    wide = width // pieces

    def loaded(i):
        part = (slice(None), pl.ds(i * wide, wide))
        return pltpu.make_async_copy(tokens_ref.at[part], tokens.at[part], got.at[i])

    def stored(i):
        part = (slice(None), pl.ds(i * wide, wide))
        return pltpu.make_async_copy(rows_out.at[part], out_ref.at[part], put.at[i])

    ids_copy = pltpu.make_async_copy(ids_in, ids_ref, first)
    ids_copy.start()
    for i in range(pieces):
        loaded(i).start()
    ids_copy.wait()
    key = slot_keys(ids_ref, experts)
    all_keys = times(ones_where(iota((rows, experts), 0) // each == iota((rows, experts), 1)), key)
    place = (iota((rows, count), 0) % each + each * chunk).astype(jnp.float32)
    pick[...] = ones_where(all_keys == place)
    for i in range(pieces):
        loaded(i).wait()
        part = tokens[:, i * wide : (i + 1) * wide]
        rows_out[:, i * wide : (i + 1) * wide] = times(pick[...], part).astype(jnp.bfloat16)
        stored(i).start()
    for i in range(pieces):
        stored(i).wait()


def slots_of_tokens(tokens, turned_ids, experts, slots, chunk):
    count, width = tokens.shape
    rows = experts * slots // CHUNKS
    return pl.pallas_call(
        functools.partial(pick_kernel, experts, chunk),
        name="pick_slots",
        out_shape=jax.ShapeDtypeStruct((rows, width), jnp.bfloat16),
        in_specs=[pl.BlockSpec(memory_space=pl.ANY)] * 2,
        out_specs=pl.BlockSpec(memory_space=pl.ANY),
        scratch_shapes=[
            pltpu.VMEM((TOP, count), jnp.int32),
            pltpu.VMEM((count, width), jnp.bfloat16),
            pltpu.VMEM((rows, width), jnp.bfloat16),
            pltpu.VMEM((rows, count), jnp.bfloat16),
            pltpu.SemaphoreType.DMA((PIECES,)),
            pltpu.SemaphoreType.DMA((PIECES,)),
            pltpu.SemaphoreType.DMA,
        ],
        compiler_params=pltpu.CompilerParams(vmem_limit_bytes=VMEM_BYTES),
    )(turned_ids, tokens)


def expert_kernel(
    steps,
    x_ref,
    g0,
    g1,
    u0,
    u1,
    d0,
    d1,
    out_ref,
    gate0,
    gate1,
    up0,
    up1,
    hid0,
    hid1,
    gather,
    spread,
    spread3,
):
    step = pl.program_id(0)
    pairs = ((gate0, g0), (gate1, g1), (up0, u0), (up1, u1))

    @pl.when(step == 0)
    def _():
        for total, _w in pairs:
            total[...] = jnp.zeros_like(total)
        width, blocks = gather.shape
        gather[...] = ones_where(iota((width, blocks), 0) == BLOCK * iota((width, blocks), 1))
        spread[...] = ones_where(iota((blocks, width), 1) // BLOCK == iota((blocks, width), 0))
        for j in range(3):
            spread3[j * blocks : (j + 1) * blocks, :] = spread[...]

    @pl.when(step < steps)
    def _():
        x = restored_rows(x_ref[...], gather[...], spread[...], spread3[...])
        for total, w in pairs:
            total[...] += jnp.dot(x, w[...], preferred_element_type=jnp.float32)

    @pl.when(step == steps - 1)
    def _():
        for hid, gate, up in ((hid0, gate0, up0), (hid1, gate1, up1)):
            v = gate[...]
            hid[...] = (v / (1.0 + jnp.exp(-v)) * up[...]).astype(jnp.bfloat16)

    @pl.when(step >= steps)
    def _():
        out_ref[...] = (
            jnp.dot(hid0[...], d0[...], preferred_element_type=jnp.float32)
            + jnp.dot(hid1[...], d1[...], preferred_element_type=jnp.float32)
        ).astype(jnp.bfloat16)


def expert(rows, gates, ups, downs):
    count, width = rows.shape
    half = gates[0].shape[-1]
    wide = 1024
    steps = width // wide
    first = lambda s: jnp.minimum(s, steps - 1)
    second = lambda s: jnp.maximum(s - steps, 0)
    into = pl.BlockSpec((None, wide, half), lambda s: (0, first(s), 0))
    out_of = pl.BlockSpec((None, half, wide), lambda s: (0, 0, second(s)))
    return pl.pallas_call(
        functools.partial(expert_kernel, steps),
        name="expert_rows",
        out_shape=jax.ShapeDtypeStruct((count, width), jnp.bfloat16),
        grid=(2 * steps,),
        in_specs=[pl.BlockSpec((count, wide), lambda s: (0, first(s)))] + [into] * 4 + [out_of] * 2,
        out_specs=pl.BlockSpec((count, wide), lambda s: (0, second(s))),
        scratch_shapes=[pltpu.VMEM((count, half), jnp.float32)] * 4
        + [pltpu.VMEM((count, half), jnp.bfloat16)] * 2
        + [
            pltpu.VMEM((wide, wide // BLOCK), jnp.bfloat16),
            pltpu.VMEM((wide // BLOCK, wide), jnp.bfloat16),
            pltpu.VMEM((3 * wide // BLOCK, wide), jnp.bfloat16),
        ],
        compiler_params=pltpu.CompilerParams(
            dimension_semantics=("arbitrary",), vmem_limit_bytes=VMEM_BYTES
        ),
        cost_estimate=pl.CostEstimate(
            flops=count * width * half * 12,
            transcendentals=count * half * 2,
            bytes_accessed=width * half * 12 + count * width * 4,
        ),
    )(rows, *gates, *ups, *downs)


def table_kernel(experts, chunks, ids_ref, affinity_ref, *out_refs):
    count = ids_ref.shape[1]
    rows = out_refs[0].shape[1]
    each = rows // experts
    key = slot_keys(ids_ref, experts)
    total = affinity_ref[0:1, :]
    for k in range(1, TOP):
        total = total + affinity_ref[k : k + 1, :]
    row = iota((experts, count), 0)
    weight = jnp.zeros((experts, count), jnp.float32)
    for k in range(TOP):
        share = affinity_ref[k : k + 1, :] / total
        weight = jnp.where(ids_ref[k : k + 1, :] == row, share, weight)
    same = ones_where(iota((count, count), 0) == iota((count, count), 1))
    spread = ones_where(iota((experts, rows), 1) // each == iota((experts, rows), 0))

    def by_token(value):
        turned = lax.dot_general(
            same, value, (((1,), (1,)), ((), ())), preferred_element_type=jnp.float32
        )
        return times(turned.astype(jnp.bfloat16), spread)

    wide = by_token(key)
    upper, lower = [by_token(part) for part in halves(weight)]
    place = (iota((count, rows), 1) % each).astype(jnp.float32)
    for j in range(chunks):
        hit = wide == place + float(each * j)
        out_refs[j][0:count, :] = jnp.where(hit, upper, 0.0).astype(jnp.bfloat16)
        out_refs[j][count : 2 * count, :] = jnp.where(hit, lower, 0.0).astype(jnp.bfloat16)


def weights_of_slots(turned_ids, turned_affinity, experts, slots, chunks):
    count = turned_ids.shape[1]
    rows = experts * slots // chunks
    return pl.pallas_call(
        functools.partial(table_kernel, experts, chunks),
        name="slot_weights",
        out_shape=[jax.ShapeDtypeStruct((2 * count, rows), jnp.bfloat16)] * chunks,
    )(turned_ids, turned_affinity)


def mix_kernel(table_ref, in_ref, *rest):
    known_refs, out_ref = rest[:-7], rest[-7]
    values, mixed, known, got, put, held = rest[-6:]
    count, width = mixed.shape
    pieces = put.shape[0]
    wide = width // pieces

    def part(i):
        return (slice(None), pl.ds(i * wide, wide))

    def loaded(i):
        return pltpu.make_async_copy(in_ref.at[part(i)], values.at[part(i)], got.at[i])

    def stored(i):
        return pltpu.make_async_copy(mixed.at[part(i)], out_ref.at[part(i)], put.at[i])

    def kept(i):
        return pltpu.make_async_copy(known_refs[0].at[part(i)], known.at[part(i)], held.at[i])

    for i in range(pieces):
        loaded(i).start()
        if known_refs:
            kept(i).start()
    for i in range(pieces):
        loaded(i).wait()
        both = times(table_ref[...], values[:, i * wide : (i + 1) * wide])
        total = both[:count] + both[count:]
        if known_refs:
            kept(i).wait()
            total = total + known[:, i * wide : (i + 1) * wide].astype(jnp.float32)
        mixed[:, i * wide : (i + 1) * wide] = total.astype(mixed.dtype)
        stored(i).start()
    for i in range(pieces):
        stored(i).wait()


def mix(table, rows, known):
    count = table.shape[0] // 2
    slots, width = rows.shape
    anywhere = pl.BlockSpec(memory_space=pl.ANY)
    vmem = pl.BlockSpec(memory_space=pltpu.VMEM)
    return pl.pallas_call(
        mix_kernel,
        name="mix_slots",
        out_shape=jax.ShapeDtypeStruct((count, width), jnp.bfloat16),
        in_specs=[vmem, anywhere] + [anywhere] * len(known),
        out_specs=anywhere,
        scratch_shapes=[
            pltpu.VMEM((slots, width), jnp.bfloat16),
            pltpu.VMEM((count, width), jnp.bfloat16),
            pltpu.VMEM((count, width), jnp.bfloat16),
            pltpu.SemaphoreType.DMA((PIECES,)),
            pltpu.SemaphoreType.DMA((PIECES,)),
            pltpu.SemaphoreType.DMA((PIECES,)),
        ],
        compiler_params=pltpu.CompilerParams(vmem_limit_bytes=VMEM_BYTES),
        cost_estimate=pl.CostEstimate(
            flops=4 * count * slots * width, transcendentals=0, bytes_accessed=2 * slots * width
        ),
    )(table, rows, *known)


def exchange(rows, devices):
    count, width = rows.shape
    split = rows.reshape(devices, count // devices, width)
    return lax.all_to_all(split, "ep", split_axis=0, concat_axis=0, tiled=True).reshape(
        count, width
    )


def on_device(tokens, expert_ids, affinity, w_gate, w_up, w_down):
    devices = lax.axis_size("ep")
    experts = devices // 2
    slots = 2 * tokens.shape[0] * TOP // experts
    pairs = [(s, s ^ 1) for s in range(devices)]
    gates, ups, downs = [(w, lax.ppermute(w, "ep", pairs)) for w in (w_gate, w_up, w_down)]
    turned_ids = expert_ids.T
    table = weights_of_slots(turned_ids, affinity.T, experts, slots, CHUNKS)
    parts = []
    for chunk in range(CHUNKS):
        rows = exchange(slots_of_tokens(tokens, turned_ids, experts, slots, chunk), devices)
        parts.append(exchange(expert(rows, gates, ups, downs), devices))
    known = []
    for chunk in range(CHUNKS - 1):
        known = [mix(table[chunk], parts[chunk], known)]
    return mix(table[CHUNKS - 1], parts[CHUNKS - 1], known)


def solution(mesh):
    rows = P(("dp", "ep"), None)
    weights = P("ep", None, None)
    return jax.shard_map(
        on_device,
        mesh=mesh,
        in_specs=(rows, rows, rows, weights, weights, weights),
        out_specs=rows,
        check_vma=False,
    )
```

```python
import functools
import jax
import jax.numpy as jnp
from jax import lax
from jax.experimental import pallas as pl
from jax.experimental.pallas import tpu as pltpu
from jax.sharding import PartitionSpec as P

TOP = 2
BLOCK = 16
LANES = 128
CHUNKS = 2
PIECES = 7
VMEM_BYTES = 56 * 1024 * 1024


def iota(shape, dim):
    return lax.broadcasted_iota(jnp.int32, shape, dim)


def halves(value):
    upper = value.astype(jnp.bfloat16)
    return upper, (value - upper.astype(jnp.float32)).astype(jnp.bfloat16)


def ones_where(hit):
    return hit.astype(jnp.float32).astype(jnp.bfloat16)


def times(a, b):
    return jnp.dot(a, b, preferred_element_type=jnp.float32)


def slot_keys(turned_ids_ref, experts):
    count = turned_ids_ref.shape[1]
    row = iota((experts, count), 0)
    hit = turned_ids_ref[0:1, :] == row
    for k in range(1, TOP):
        hit = hit | (turned_ids_ref[k : k + 1, :] == row)
    earlier = ones_where(iota((count, count), 0) < iota((count, count), 1))
    rank = times(ones_where(hit), earlier)
    return jnp.where(hit, rank, -1.0).astype(jnp.bfloat16)


def restored_rows(tokens, gather, spread, spread3):
    x = tokens.astype(jnp.float32)
    width = x.shape[1]
    tops = []
    for at in range(0, width, LANES):
        top = jnp.abs(x[:, at : at + LANES])
        for step in (1, 2, 4, 8):
            top = jnp.maximum(top, pltpu.roll(top, LANES - step, 1))
        tops.append(top.astype(jnp.bfloat16))
    largest = times(jnp.concatenate(tops, axis=1), gather)
    scale = (jnp.maximum(largest, 0.25) / 9.0).astype(jnp.bfloat16)
    inverse = 1.0 / scale.astype(jnp.float32)
    first, rest = halves(inverse)
    second, third = halves(inverse - first.astype(jnp.float32))
    inverse = times(jnp.concatenate([first, second, third], axis=1), spread3)
    scale = times(scale, spread)
    payload = jnp.clip(x * inverse, -6.0, 6.0).astype(jnp.bfloat16).astype(jnp.float32)
    return (payload * scale).astype(jnp.bfloat16)


def pick_kernel(
    experts, chunk, ids_in, tokens_ref, out_ref, ids_ref, tokens, rows_out, pick, got, put, first
):
    count, width = tokens.shape
    rows = rows_out.shape[0]
    each = rows // experts
    pieces = got.shape[0]
    wide = width // pieces

    def loaded(i):
        part = (slice(None), pl.ds(i * wide, wide))
        return pltpu.make_async_copy(tokens_ref.at[part], tokens.at[part], got.at[i])

    def stored(i):
        part = (slice(None), pl.ds(i * wide, wide))
        return pltpu.make_async_copy(rows_out.at[part], out_ref.at[part], put.at[i])

    ids_copy = pltpu.make_async_copy(ids_in, ids_ref, first)
    ids_copy.start()
    for i in range(pieces):
        loaded(i).start()
    ids_copy.wait()
    key = slot_keys(ids_ref, experts)
    all_keys = times(ones_where(iota((rows, experts), 0) // each == iota((rows, experts), 1)), key)
    place = (iota((rows, count), 0) % each + each * chunk).astype(jnp.float32)
    pick[...] = ones_where(all_keys == place)
    for i in range(pieces):
        loaded(i).wait()
        part = tokens[:, i * wide : (i + 1) * wide]
        rows_out[:, i * wide : (i + 1) * wide] = times(pick[...], part).astype(jnp.bfloat16)
        stored(i).start()
    for i in range(pieces):
        stored(i).wait()


def slots_of_tokens(tokens, turned_ids, experts, slots, chunk):
    count, width = tokens.shape
    rows = experts * slots // CHUNKS
    return pl.pallas_call(
        functools.partial(pick_kernel, experts, chunk),
        name="pick_slots",
        out_shape=jax.ShapeDtypeStruct((rows, width), jnp.bfloat16),
        in_specs=[pl.BlockSpec(memory_space=pl.ANY)] * 2,
        out_specs=pl.BlockSpec(memory_space=pl.ANY),
        scratch_shapes=[
            pltpu.VMEM((TOP, count), jnp.int32),
            pltpu.VMEM((count, width), jnp.bfloat16),
            pltpu.VMEM((rows, width), jnp.bfloat16),
            pltpu.VMEM((rows, count), jnp.bfloat16),
            pltpu.SemaphoreType.DMA((PIECES,)),
            pltpu.SemaphoreType.DMA((PIECES,)),
            pltpu.SemaphoreType.DMA,
        ],
        compiler_params=pltpu.CompilerParams(vmem_limit_bytes=VMEM_BYTES),
    )(turned_ids, tokens)


def expert_kernel(
    steps,
    x_ref,
    g0,
    g1,
    u0,
    u1,
    d0,
    d1,
    out_ref,
    gate0,
    gate1,
    up0,
    up1,
    hid0,
    hid1,
    gather,
    spread,
    spread3,
):
    step = pl.program_id(0)
    pairs = ((gate0, g0), (gate1, g1), (up0, u0), (up1, u1))

    @pl.when(step == 0)
    def _():
        for total, _w in pairs:
            total[...] = jnp.zeros_like(total)
        width, blocks = gather.shape
        gather[...] = ones_where(iota((width, blocks), 0) == BLOCK * iota((width, blocks), 1))
        spread[...] = ones_where(iota((blocks, width), 1) // BLOCK == iota((blocks, width), 0))
        for j in range(3):
            spread3[j * blocks : (j + 1) * blocks, :] = spread[...]

    @pl.when(step < steps)
    def _():
        x = restored_rows(x_ref[...], gather[...], spread[...], spread3[...])
        for total, w in pairs:
            total[...] += jnp.dot(x, w[...], preferred_element_type=jnp.float32)

    @pl.when(step == steps - 1)
    def _():
        for hid, gate, up in ((hid0, gate0, up0), (hid1, gate1, up1)):
            v = gate[...]
            hid[...] = (v / (1.0 + jnp.exp(-v)) * up[...]).astype(jnp.bfloat16)

    @pl.when(step >= steps)
    def _():
        out_ref[...] = (
            jnp.dot(hid0[...], d0[...], preferred_element_type=jnp.float32)
            + jnp.dot(hid1[...], d1[...], preferred_element_type=jnp.float32)
        ).astype(jnp.bfloat16)


def expert(rows, gates, ups, downs):
    count, width = rows.shape
    half = gates[0].shape[-1]
    wide = 1024
    steps = width // wide
    first = lambda s: jnp.minimum(s, steps - 1)
    second = lambda s: jnp.maximum(s - steps, 0)
    into = pl.BlockSpec((None, wide, half), lambda s: (0, first(s), 0))
    out_of = pl.BlockSpec((None, half, wide), lambda s: (0, 0, second(s)))
    return pl.pallas_call(
        functools.partial(expert_kernel, steps),
        name="expert_rows",
        out_shape=jax.ShapeDtypeStruct((count, width), jnp.bfloat16),
        grid=(2 * steps,),
        in_specs=[pl.BlockSpec((count, wide), lambda s: (0, first(s)))] + [into] * 4 + [out_of] * 2,
        out_specs=pl.BlockSpec((count, wide), lambda s: (0, second(s))),
        scratch_shapes=[pltpu.VMEM((count, half), jnp.float32)] * 4
        + [pltpu.VMEM((count, half), jnp.bfloat16)] * 2
        + [
            pltpu.VMEM((wide, wide // BLOCK), jnp.bfloat16),
            pltpu.VMEM((wide // BLOCK, wide), jnp.bfloat16),
            pltpu.VMEM((3 * wide // BLOCK, wide), jnp.bfloat16),
        ],
        compiler_params=pltpu.CompilerParams(
            dimension_semantics=("arbitrary",), vmem_limit_bytes=VMEM_BYTES
        ),
        cost_estimate=pl.CostEstimate(
            flops=count * width * half * 12,
            transcendentals=count * half * 2,
            bytes_accessed=width * half * 12 + count * width * 4,
        ),
    )(rows, *gates, *ups, *downs)


def table_kernel(experts, chunks, ids_ref, affinity_ref, *out_refs):
    count = ids_ref.shape[1]
    rows = out_refs[0].shape[1]
    each = rows // experts
    key = slot_keys(ids_ref, experts)
    total = affinity_ref[0:1, :]
    for k in range(1, TOP):
        total = total + affinity_ref[k : k + 1, :]
    row = iota((experts, count), 0)
    weight = jnp.zeros((experts, count), jnp.float32)
    for k in range(TOP):
        share = affinity_ref[k : k + 1, :] / total
        weight = jnp.where(ids_ref[k : k + 1, :] == row, share, weight)
    same = ones_where(iota((count, count), 0) == iota((count, count), 1))
    spread = ones_where(iota((experts, rows), 1) // each == iota((experts, rows), 0))

    def by_token(value):
        turned = lax.dot_general(
            same, value, (((1,), (1,)), ((), ())), preferred_element_type=jnp.float32
        )
        return times(turned.astype(jnp.bfloat16), spread)

    wide = by_token(key)
    upper, lower = [by_token(part) for part in halves(weight)]
    place = (iota((count, rows), 1) % each).astype(jnp.float32)
    for j in range(chunks):
        hit = wide == place + float(each * j)
        out_refs[j][0:count, :] = jnp.where(hit, upper, 0.0).astype(jnp.bfloat16)
        out_refs[j][count : 2 * count, :] = jnp.where(hit, lower, 0.0).astype(jnp.bfloat16)


def weights_of_slots(turned_ids, turned_affinity, experts, slots, chunks):
    count = turned_ids.shape[1]
    rows = experts * slots // chunks
    return pl.pallas_call(
        functools.partial(table_kernel, experts, chunks),
        name="slot_weights",
        out_shape=[jax.ShapeDtypeStruct((2 * count, rows), jnp.bfloat16)] * chunks,
    )(turned_ids, turned_affinity)


def mix_kernel(table_ref, in_ref, *rest):
    known_refs, out_ref = rest[:-7], rest[-7]
    values, mixed, known, got, put, held = rest[-6:]
    count, width = mixed.shape
    pieces = put.shape[0]
    wide = width // pieces

    def part(i):
        return (slice(None), pl.ds(i * wide, wide))

    def loaded(i):
        return pltpu.make_async_copy(in_ref.at[part(i)], values.at[part(i)], got.at[i])

    def stored(i):
        return pltpu.make_async_copy(mixed.at[part(i)], out_ref.at[part(i)], put.at[i])

    def kept(i):
        return pltpu.make_async_copy(known_refs[0].at[part(i)], known.at[part(i)], held.at[i])

    for i in range(pieces):
        loaded(i).start()
        if known_refs:
            kept(i).start()
    for i in range(pieces):
        loaded(i).wait()
        both = times(table_ref[...], values[:, i * wide : (i + 1) * wide])
        total = both[:count] + both[count:]
        if known_refs:
            kept(i).wait()
            total = total + known[:, i * wide : (i + 1) * wide].astype(jnp.float32)
        mixed[:, i * wide : (i + 1) * wide] = total.astype(mixed.dtype)
        stored(i).start()
    for i in range(pieces):
        stored(i).wait()


def mix(table, rows, known):
    count = table.shape[0] // 2
    slots, width = rows.shape
    anywhere = pl.BlockSpec(memory_space=pl.ANY)
    vmem = pl.BlockSpec(memory_space=pltpu.VMEM)
    return pl.pallas_call(
        mix_kernel,
        name="mix_slots",
        out_shape=jax.ShapeDtypeStruct((count, width), jnp.bfloat16),
        in_specs=[vmem, anywhere] + [anywhere] * len(known),
        out_specs=anywhere,
        scratch_shapes=[
            pltpu.VMEM((slots, width), jnp.bfloat16),
            pltpu.VMEM((count, width), jnp.bfloat16),
            pltpu.VMEM((count, width), jnp.bfloat16),
            pltpu.SemaphoreType.DMA((PIECES,)),
            pltpu.SemaphoreType.DMA((PIECES,)),
            pltpu.SemaphoreType.DMA((PIECES,)),
        ],
        compiler_params=pltpu.CompilerParams(vmem_limit_bytes=VMEM_BYTES),
        cost_estimate=pl.CostEstimate(
            flops=4 * count * slots * width, transcendentals=0, bytes_accessed=2 * slots * width
        ),
    )(table, rows, *known)


def exchange(rows, devices):
    count, width = rows.shape
    split = rows.reshape(devices, count // devices, width)
    return lax.all_to_all(split, "ep", split_axis=0, concat_axis=0, tiled=True).reshape(
        count, width
    )


def on_device(tokens, expert_ids, affinity, w_gate, w_up, w_down):
    devices = lax.axis_size("ep")
    experts = devices // 2
    slots = 2 * tokens.shape[0] * TOP // experts
    pairs = [(s, s ^ 1) for s in range(devices)]
    gates, ups = [(w, lax.ppermute(w, "ep", pairs)) for w in (w_gate, w_up)]
    turned_ids = expert_ids.T
    table = weights_of_slots(turned_ids, affinity.T, experts, slots, CHUNKS)
    parts = []
    sent = [
        slots_of_tokens(tokens, turned_ids, experts, slots, chunk) for chunk in range(CHUNKS)
    ]
    first, second, late = lax.optimization_barrier((exchange(sent[0], devices), sent[1], w_down))
    downs = (w_down, lax.ppermute(late, "ep", pairs))
    arrived = [first, exchange(second, devices)]
    for rows in arrived:
        parts.append(exchange(expert(rows, gates, ups, downs), devices))
    known = []
    for chunk in range(CHUNKS - 1):
        known = [mix(table[chunk], parts[chunk], known)]
    return mix(table[CHUNKS - 1], parts[CHUNKS - 1], known)


def solution(mesh):
    rows = P(("dp", "ep"), None)
    weights = P("ep", None, None)
    return jax.shard_map(
        on_device,
        mesh=mesh,
        in_specs=(rows, rows, rows, weights, weights, weights),
        out_specs=rows,
        check_vma=False,
    )
```

```python
import functools
import jax
import jax.numpy as jnp
from jax import lax
from jax.experimental import pallas as pl
from jax.experimental.pallas import tpu as pltpu
from jax.sharding import PartitionSpec as P

TOP = 2
BLOCK = 16
LANES = 128
CHUNKS = 2
PIECES = 14
VMEM_BYTES = 56 * 1024 * 1024


def iota(shape, dim):
    return lax.broadcasted_iota(jnp.int32, shape, dim)


def halves(value):
    upper = value.astype(jnp.bfloat16)
    return upper, (value - upper.astype(jnp.float32)).astype(jnp.bfloat16)


def ones_where(hit):
    return hit.astype(jnp.float32).astype(jnp.bfloat16)


def times(a, b):
    return jnp.dot(a, b, preferred_element_type=jnp.float32)


def slot_keys(turned_ids_ref, experts):
    count = turned_ids_ref.shape[1]
    row = iota((experts, count), 0)
    hit = turned_ids_ref[0:1, :] == row
    for k in range(1, TOP):
        hit = hit | (turned_ids_ref[k : k + 1, :] == row)
    earlier = ones_where(iota((count, count), 0) < iota((count, count), 1))
    rank = times(ones_where(hit), earlier)
    return jnp.where(hit, rank, -1.0).astype(jnp.bfloat16)


def restored_rows(tokens, gather, spread, spread3):
    x = tokens.astype(jnp.float32)
    width = x.shape[1]
    tops = []
    for at in range(0, width, LANES):
        top = jnp.abs(x[:, at : at + LANES])
        for step in (1, 2, 4, 8):
            top = jnp.maximum(top, pltpu.roll(top, LANES - step, 1))
        tops.append(top.astype(jnp.bfloat16))
    largest = times(jnp.concatenate(tops, axis=1), gather)
    scale = (jnp.maximum(largest, 0.25) / 9.0).astype(jnp.bfloat16)
    inverse = 1.0 / scale.astype(jnp.float32)
    first, rest = halves(inverse)
    second, third = halves(inverse - first.astype(jnp.float32))
    inverse = times(jnp.concatenate([first, second, third], axis=1), spread3)
    scale = times(scale, spread)
    payload = jnp.clip(x * inverse, -6.0, 6.0).astype(jnp.bfloat16).astype(jnp.float32)
    return (payload * scale).astype(jnp.bfloat16)


def pick_kernel(
    experts, chunk, ids_in, tokens_ref, out_ref, ids_ref, tokens, rows_out, pick, got, put, first
):
    count, width = tokens.shape
    rows = rows_out.shape[0]
    each = rows // experts
    pieces = got.shape[0]
    wide = width // pieces

    def loaded(i):
        part = (slice(None), pl.ds(i * wide, wide))
        return pltpu.make_async_copy(tokens_ref.at[part], tokens.at[part], got.at[i])

    def stored(i):
        part = (slice(None), pl.ds(i * wide, wide))
        return pltpu.make_async_copy(rows_out.at[part], out_ref.at[part], put.at[i])

    ids_copy = pltpu.make_async_copy(ids_in, ids_ref, first)
    ids_copy.start()
    for i in range(pieces):
        loaded(i).start()
    ids_copy.wait()
    key = slot_keys(ids_ref, experts)
    all_keys = times(ones_where(iota((rows, experts), 0) // each == iota((rows, experts), 1)), key)
    place = (iota((rows, count), 0) % each + each * chunk).astype(jnp.float32)
    pick[...] = ones_where(all_keys == place)
    for i in range(pieces):
        loaded(i).wait()
        part = tokens[:, i * wide : (i + 1) * wide]
        rows_out[:, i * wide : (i + 1) * wide] = times(pick[...], part).astype(jnp.bfloat16)
        stored(i).start()
    for i in range(pieces):
        stored(i).wait()


def slots_of_tokens(tokens, turned_ids, experts, slots, chunk):
    count, width = tokens.shape
    rows = experts * slots // CHUNKS
    return pl.pallas_call(
        functools.partial(pick_kernel, experts, chunk),
        name="pick_slots",
        out_shape=jax.ShapeDtypeStruct((rows, width), jnp.bfloat16),
        in_specs=[pl.BlockSpec(memory_space=pl.ANY)] * 2,
        out_specs=pl.BlockSpec(memory_space=pl.ANY),
        scratch_shapes=[
            pltpu.VMEM((TOP, count), jnp.int32),
            pltpu.VMEM((count, width), jnp.bfloat16),
            pltpu.VMEM((rows, width), jnp.bfloat16),
            pltpu.VMEM((rows, count), jnp.bfloat16),
            pltpu.SemaphoreType.DMA((PIECES,)),
            pltpu.SemaphoreType.DMA((PIECES,)),
            pltpu.SemaphoreType.DMA,
        ],
        compiler_params=pltpu.CompilerParams(vmem_limit_bytes=VMEM_BYTES),
    )(turned_ids, tokens)


def expert_kernel(
    steps,
    x_ref,
    g0,
    g1,
    u0,
    u1,
    d0,
    d1,
    out_ref,
    gate0,
    gate1,
    up0,
    up1,
    hid0,
    hid1,
    gather,
    spread,
    spread3,
):
    step = pl.program_id(0)
    pairs = ((gate0, g0), (gate1, g1), (up0, u0), (up1, u1))

    @pl.when(step == 0)
    def _():
        for total, _w in pairs:
            total[...] = jnp.zeros_like(total)
        width, blocks = gather.shape
        gather[...] = ones_where(iota((width, blocks), 0) == BLOCK * iota((width, blocks), 1))
        spread[...] = ones_where(iota((blocks, width), 1) // BLOCK == iota((blocks, width), 0))
        for j in range(3):
            spread3[j * blocks : (j + 1) * blocks, :] = spread[...]

    @pl.when(step < steps)
    def _():
        x = restored_rows(x_ref[...], gather[...], spread[...], spread3[...])
        for total, w in pairs:
            total[...] += jnp.dot(x, w[...], preferred_element_type=jnp.float32)

    @pl.when(step == steps - 1)
    def _():
        for hid, gate, up in ((hid0, gate0, up0), (hid1, gate1, up1)):
            v = gate[...]
            hid[...] = (v / (1.0 + jnp.exp(-v)) * up[...]).astype(jnp.bfloat16)

    @pl.when(step >= steps)
    def _():
        out_ref[...] = (
            jnp.dot(hid0[...], d0[...], preferred_element_type=jnp.float32)
            + jnp.dot(hid1[...], d1[...], preferred_element_type=jnp.float32)
        ).astype(jnp.bfloat16)


def expert(rows, gates, ups, downs):
    count, width = rows.shape
    half = gates[0].shape[-1]
    wide = 1024
    steps = width // wide
    first = lambda s: jnp.minimum(s, steps - 1)
    second = lambda s: jnp.maximum(s - steps, 0)
    into = pl.BlockSpec((None, wide, half), lambda s: (0, first(s), 0))
    out_of = pl.BlockSpec((None, half, wide), lambda s: (0, 0, second(s)))
    return pl.pallas_call(
        functools.partial(expert_kernel, steps),
        name="expert_rows",
        out_shape=jax.ShapeDtypeStruct((count, width), jnp.bfloat16),
        grid=(2 * steps,),
        in_specs=[pl.BlockSpec((count, wide), lambda s: (0, first(s)))] + [into] * 4 + [out_of] * 2,
        out_specs=pl.BlockSpec((count, wide), lambda s: (0, second(s))),
        scratch_shapes=[pltpu.VMEM((count, half), jnp.float32)] * 4
        + [pltpu.VMEM((count, half), jnp.bfloat16)] * 2
        + [
            pltpu.VMEM((wide, wide // BLOCK), jnp.bfloat16),
            pltpu.VMEM((wide // BLOCK, wide), jnp.bfloat16),
            pltpu.VMEM((3 * wide // BLOCK, wide), jnp.bfloat16),
        ],
        compiler_params=pltpu.CompilerParams(
            dimension_semantics=("arbitrary",), vmem_limit_bytes=VMEM_BYTES
        ),
        cost_estimate=pl.CostEstimate(
            flops=count * width * half * 12,
            transcendentals=count * half * 2,
            bytes_accessed=width * half * 12 + count * width * 4,
        ),
    )(rows, *gates, *ups, *downs)


def table_kernel(experts, chunks, ids_ref, affinity_ref, *out_refs):
    count = ids_ref.shape[1]
    rows = out_refs[0].shape[1]
    each = rows // experts
    key = slot_keys(ids_ref, experts)
    total = affinity_ref[0:1, :]
    for k in range(1, TOP):
        total = total + affinity_ref[k : k + 1, :]
    row = iota((experts, count), 0)
    weight = jnp.zeros((experts, count), jnp.float32)
    for k in range(TOP):
        share = affinity_ref[k : k + 1, :] / total
        weight = jnp.where(ids_ref[k : k + 1, :] == row, share, weight)
    same = ones_where(iota((count, count), 0) == iota((count, count), 1))
    spread = ones_where(iota((experts, rows), 1) // each == iota((experts, rows), 0))

    def by_token(value):
        turned = lax.dot_general(
            same, value, (((1,), (1,)), ((), ())), preferred_element_type=jnp.float32
        )
        return times(turned.astype(jnp.bfloat16), spread)

    wide = by_token(key)
    upper, lower = [by_token(part) for part in halves(weight)]
    place = (iota((count, rows), 1) % each).astype(jnp.float32)
    for j in range(chunks):
        hit = wide == place + float(each * j)
        out_refs[j][0:count, :] = jnp.where(hit, upper, 0.0).astype(jnp.bfloat16)
        out_refs[j][count : 2 * count, :] = jnp.where(hit, lower, 0.0).astype(jnp.bfloat16)


def weights_of_slots(turned_ids, turned_affinity, experts, slots, chunks):
    count = turned_ids.shape[1]
    rows = experts * slots // chunks
    return pl.pallas_call(
        functools.partial(table_kernel, experts, chunks),
        name="slot_weights",
        out_shape=[jax.ShapeDtypeStruct((2 * count, rows), jnp.bfloat16)] * chunks,
    )(turned_ids, turned_affinity)


def mix_kernel(table_ref, in_ref, *rest):
    known_refs, out_ref = rest[:-7], rest[-7]
    values, mixed, known, got, put, held = rest[-6:]
    count, width = mixed.shape
    pieces = put.shape[0]
    wide = width // pieces

    def part(i):
        return (slice(None), pl.ds(i * wide, wide))

    def loaded(i):
        return pltpu.make_async_copy(in_ref.at[part(i)], values.at[part(i)], got.at[i])

    def stored(i):
        return pltpu.make_async_copy(mixed.at[part(i)], out_ref.at[part(i)], put.at[i])

    def kept(i):
        return pltpu.make_async_copy(known_refs[0].at[part(i)], known.at[part(i)], held.at[i])

    for i in range(pieces):
        loaded(i).start()
        if known_refs:
            kept(i).start()
    for i in range(pieces):
        loaded(i).wait()
        both = times(table_ref[...], values[:, i * wide : (i + 1) * wide])
        total = both[:count] + both[count:]
        if known_refs:
            kept(i).wait()
            total = total + known[:, i * wide : (i + 1) * wide].astype(jnp.float32)
        mixed[:, i * wide : (i + 1) * wide] = total.astype(mixed.dtype)
        stored(i).start()
    for i in range(pieces):
        stored(i).wait()


def mix(table, rows, known):
    count = table.shape[0] // 2
    slots, width = rows.shape
    anywhere = pl.BlockSpec(memory_space=pl.ANY)
    vmem = pl.BlockSpec(memory_space=pltpu.VMEM)
    return pl.pallas_call(
        mix_kernel,
        name="mix_slots",
        out_shape=jax.ShapeDtypeStruct((count, width), jnp.bfloat16),
        in_specs=[vmem, anywhere] + [anywhere] * len(known),
        out_specs=anywhere,
        scratch_shapes=[
            pltpu.VMEM((slots, width), jnp.bfloat16),
            pltpu.VMEM((count, width), jnp.bfloat16),
            pltpu.VMEM((count, width), jnp.bfloat16),
            pltpu.SemaphoreType.DMA((PIECES,)),
            pltpu.SemaphoreType.DMA((PIECES,)),
            pltpu.SemaphoreType.DMA((PIECES,)),
        ],
        compiler_params=pltpu.CompilerParams(vmem_limit_bytes=VMEM_BYTES),
        cost_estimate=pl.CostEstimate(
            flops=4 * count * slots * width, transcendentals=0, bytes_accessed=2 * slots * width
        ),
    )(table, rows, *known)


def exchange(rows, devices):
    count, width = rows.shape
    split = rows.reshape(devices, count // devices, width)
    return lax.all_to_all(split, "ep", split_axis=0, concat_axis=0, tiled=True).reshape(
        count, width
    )


def on_device(tokens, expert_ids, affinity, w_gate, w_up, w_down):
    devices = lax.axis_size("ep")
    experts = devices // 2
    slots = 2 * tokens.shape[0] * TOP // experts
    pairs = [(s, s ^ 1) for s in range(devices)]
    gates, ups = [(w, lax.ppermute(w, "ep", pairs)) for w in (w_gate, w_up)]
    turned_ids = expert_ids.T
    table = weights_of_slots(turned_ids, affinity.T, experts, slots, CHUNKS)
    parts = []
    sent = [
        slots_of_tokens(tokens, turned_ids, experts, slots, chunk) for chunk in range(CHUNKS)
    ]
    first, second, late = lax.optimization_barrier((exchange(sent[0], devices), sent[1], w_down))
    downs = (w_down, lax.ppermute(late, "ep", pairs))
    arrived = [first, exchange(second, devices)]
    for rows in arrived:
        parts.append(exchange(expert(rows, gates, ups, downs), devices))
    known = []
    for chunk in range(CHUNKS - 1):
        known = [mix(table[chunk], parts[chunk], known)]
    return mix(table[CHUNKS - 1], parts[CHUNKS - 1], known)


def solution(mesh):
    rows = P(("dp", "ep"), None)
    weights = P("ep", None, None)
    return jax.shard_map(
        on_device,
        mesh=mesh,
        in_specs=(rows, rows, rows, weights, weights, weights),
        out_specs=rows,
        check_vma=False,
    )
```

```python
import functools
import jax
import jax.numpy as jnp
from jax import lax
from jax.experimental import pallas as pl
from jax.experimental.pallas import tpu as pltpu
from jax.sharding import PartitionSpec as P

TOP = 2
BLOCK = 16
LANES = 128
CHUNKS = 2
PIECES = 4
VMEM_BYTES = 56 * 1024 * 1024


def iota(shape, dim):
    return lax.broadcasted_iota(jnp.int32, shape, dim)


def halves(value):
    upper = value.astype(jnp.bfloat16)
    return upper, (value - upper.astype(jnp.float32)).astype(jnp.bfloat16)


def ones_where(hit):
    return hit.astype(jnp.float32).astype(jnp.bfloat16)


def times(a, b):
    return jnp.dot(a, b, preferred_element_type=jnp.float32)


def slot_keys(turned_ids_ref, experts):
    count = turned_ids_ref.shape[1]
    row = iota((experts, count), 0)
    hit = turned_ids_ref[0:1, :] == row
    for k in range(1, TOP):
        hit = hit | (turned_ids_ref[k : k + 1, :] == row)
    earlier = ones_where(iota((count, count), 0) < iota((count, count), 1))
    rank = times(ones_where(hit), earlier)
    return jnp.where(hit, rank, -1.0).astype(jnp.bfloat16)


def restored_rows(tokens, gather, spread, spread3):
    x = tokens.astype(jnp.float32)
    width = x.shape[1]
    tops = []
    for at in range(0, width, LANES):
        top = jnp.abs(x[:, at : at + LANES])
        for step in (1, 2, 4, 8):
            top = jnp.maximum(top, pltpu.roll(top, LANES - step, 1))
        tops.append(top.astype(jnp.bfloat16))
    largest = times(jnp.concatenate(tops, axis=1), gather)
    scale = (jnp.maximum(largest, 0.25) / 9.0).astype(jnp.bfloat16)
    inverse = 1.0 / scale.astype(jnp.float32)
    first, rest = halves(inverse)
    second, third = halves(inverse - first.astype(jnp.float32))
    inverse = times(jnp.concatenate([first, second, third], axis=1), spread3)
    scale = times(scale, spread)
    payload = jnp.clip(x * inverse, -6.0, 6.0).astype(jnp.bfloat16).astype(jnp.float32)
    return (payload * scale).astype(jnp.bfloat16)


def pick_kernel(
    experts, chunk, ids_in, tokens_ref, out_ref, ids_ref, tokens, rows_out, pick, got, put, first
):
    count, width = tokens.shape
    rows = rows_out.shape[0]
    each = rows // experts
    pieces = got.shape[0]
    wide = width // pieces

    def loaded(i):
        part = (slice(None), pl.ds(i * wide, wide))
        return pltpu.make_async_copy(tokens_ref.at[part], tokens.at[part], got.at[i])

    def stored(i):
        part = (slice(None), pl.ds(i * wide, wide))
        return pltpu.make_async_copy(rows_out.at[part], out_ref.at[part], put.at[i])

    ids_copy = pltpu.make_async_copy(ids_in, ids_ref, first)
    ids_copy.start()
    for i in range(pieces):
        loaded(i).start()
    ids_copy.wait()
    key = slot_keys(ids_ref, experts)
    all_keys = times(ones_where(iota((rows, experts), 0) // each == iota((rows, experts), 1)), key)
    place = (iota((rows, count), 0) % each + each * chunk).astype(jnp.float32)
    pick[...] = ones_where(all_keys == place)
    for i in range(pieces):
        loaded(i).wait()
        part = tokens[:, i * wide : (i + 1) * wide]
        rows_out[:, i * wide : (i + 1) * wide] = times(pick[...], part).astype(jnp.bfloat16)
        stored(i).start()
    for i in range(pieces):
        stored(i).wait()


def slots_of_tokens(tokens, turned_ids, experts, slots, chunk):
    count, width = tokens.shape
    rows = experts * slots // CHUNKS
    return pl.pallas_call(
        functools.partial(pick_kernel, experts, chunk),
        name="pick_slots",
        out_shape=jax.ShapeDtypeStruct((rows, width), jnp.bfloat16),
        in_specs=[pl.BlockSpec(memory_space=pl.ANY)] * 2,
        out_specs=pl.BlockSpec(memory_space=pl.ANY),
        scratch_shapes=[
            pltpu.VMEM((TOP, count), jnp.int32),
            pltpu.VMEM((count, width), jnp.bfloat16),
            pltpu.VMEM((rows, width), jnp.bfloat16),
            pltpu.VMEM((rows, count), jnp.bfloat16),
            pltpu.SemaphoreType.DMA((PIECES,)),
            pltpu.SemaphoreType.DMA((PIECES,)),
            pltpu.SemaphoreType.DMA,
        ],
        compiler_params=pltpu.CompilerParams(vmem_limit_bytes=VMEM_BYTES),
    )(turned_ids, tokens)


def expert_kernel(
    steps,
    x_ref,
    g0,
    g1,
    u0,
    u1,
    d0,
    d1,
    out_ref,
    gate0,
    gate1,
    up0,
    up1,
    hid0,
    hid1,
    gather,
    spread,
    spread3,
):
    step = pl.program_id(0)
    pairs = ((gate0, g0), (gate1, g1), (up0, u0), (up1, u1))

    @pl.when(step == 0)
    def _():
        for total, _w in pairs:
            total[...] = jnp.zeros_like(total)
        width, blocks = gather.shape
        gather[...] = ones_where(iota((width, blocks), 0) == BLOCK * iota((width, blocks), 1))
        spread[...] = ones_where(iota((blocks, width), 1) // BLOCK == iota((blocks, width), 0))
        for j in range(3):
            spread3[j * blocks : (j + 1) * blocks, :] = spread[...]

    @pl.when(step < steps)
    def _():
        x = restored_rows(x_ref[...], gather[...], spread[...], spread3[...])
        for total, w in pairs:
            total[...] += jnp.dot(x, w[...], preferred_element_type=jnp.float32)

    @pl.when(step == steps - 1)
    def _():
        for hid, gate, up in ((hid0, gate0, up0), (hid1, gate1, up1)):
            v = gate[...]
            hid[...] = (v / (1.0 + jnp.exp(-v)) * up[...]).astype(jnp.bfloat16)

    @pl.when(step >= steps)
    def _():
        out_ref[...] = (
            jnp.dot(hid0[...], d0[...], preferred_element_type=jnp.float32)
            + jnp.dot(hid1[...], d1[...], preferred_element_type=jnp.float32)
        ).astype(jnp.bfloat16)


def expert(rows, gates, ups, downs):
    count, width = rows.shape
    half = gates[0].shape[-1]
    wide = 1024
    steps = width // wide
    first = lambda s: jnp.minimum(s, steps - 1)
    second = lambda s: jnp.maximum(s - steps, 0)
    into = pl.BlockSpec((None, wide, half), lambda s: (0, first(s), 0))
    out_of = pl.BlockSpec((None, half, wide), lambda s: (0, 0, second(s)))
    return pl.pallas_call(
        functools.partial(expert_kernel, steps),
        name="expert_rows",
        out_shape=jax.ShapeDtypeStruct((count, width), jnp.bfloat16),
        grid=(2 * steps,),
        in_specs=[pl.BlockSpec((count, wide), lambda s: (0, first(s)))] + [into] * 4 + [out_of] * 2,
        out_specs=pl.BlockSpec((count, wide), lambda s: (0, second(s))),
        scratch_shapes=[pltpu.VMEM((count, half), jnp.float32)] * 4
        + [pltpu.VMEM((count, half), jnp.bfloat16)] * 2
        + [
            pltpu.VMEM((wide, wide // BLOCK), jnp.bfloat16),
            pltpu.VMEM((wide // BLOCK, wide), jnp.bfloat16),
            pltpu.VMEM((3 * wide // BLOCK, wide), jnp.bfloat16),
        ],
        compiler_params=pltpu.CompilerParams(
            dimension_semantics=("arbitrary",), vmem_limit_bytes=VMEM_BYTES
        ),
        cost_estimate=pl.CostEstimate(
            flops=count * width * half * 12,
            transcendentals=count * half * 2,
            bytes_accessed=width * half * 12 + count * width * 4,
        ),
    )(rows, *gates, *ups, *downs)


def table_kernel(experts, chunks, ids_ref, affinity_ref, *out_refs):
    count = ids_ref.shape[1]
    rows = out_refs[0].shape[1]
    each = rows // experts
    key = slot_keys(ids_ref, experts)
    total = affinity_ref[0:1, :]
    for k in range(1, TOP):
        total = total + affinity_ref[k : k + 1, :]
    row = iota((experts, count), 0)
    weight = jnp.zeros((experts, count), jnp.float32)
    for k in range(TOP):
        share = affinity_ref[k : k + 1, :] / total
        weight = jnp.where(ids_ref[k : k + 1, :] == row, share, weight)
    same = ones_where(iota((count, count), 0) == iota((count, count), 1))
    spread = ones_where(iota((experts, rows), 1) // each == iota((experts, rows), 0))

    def by_token(value):
        turned = lax.dot_general(
            same, value, (((1,), (1,)), ((), ())), preferred_element_type=jnp.float32
        )
        return times(turned.astype(jnp.bfloat16), spread)

    wide = by_token(key)
    upper, lower = [by_token(part) for part in halves(weight)]
    place = (iota((count, rows), 1) % each).astype(jnp.float32)
    for j in range(chunks):
        hit = wide == place + float(each * j)
        out_refs[j][0:count, :] = jnp.where(hit, upper, 0.0).astype(jnp.bfloat16)
        out_refs[j][count : 2 * count, :] = jnp.where(hit, lower, 0.0).astype(jnp.bfloat16)


def weights_of_slots(turned_ids, turned_affinity, experts, slots, chunks):
    count = turned_ids.shape[1]
    rows = experts * slots // chunks
    return pl.pallas_call(
        functools.partial(table_kernel, experts, chunks),
        name="slot_weights",
        out_shape=[jax.ShapeDtypeStruct((2 * count, rows), jnp.bfloat16)] * chunks,
    )(turned_ids, turned_affinity)


def mix_kernel(table_ref, in_ref, *rest):
    known_refs, out_ref = rest[:-7], rest[-7]
    values, mixed, known, got, put, held = rest[-6:]
    count, width = mixed.shape
    pieces = put.shape[0]
    wide = width // pieces

    def part(i):
        return (slice(None), pl.ds(i * wide, wide))

    def loaded(i):
        return pltpu.make_async_copy(in_ref.at[part(i)], values.at[part(i)], got.at[i])

    def stored(i):
        return pltpu.make_async_copy(mixed.at[part(i)], out_ref.at[part(i)], put.at[i])

    def kept(i):
        return pltpu.make_async_copy(known_refs[0].at[part(i)], known.at[part(i)], held.at[i])

    for i in range(pieces):
        loaded(i).start()
        if known_refs:
            kept(i).start()
    for i in range(pieces):
        loaded(i).wait()
        both = times(table_ref[...], values[:, i * wide : (i + 1) * wide])
        total = both[:count] + both[count:]
        if known_refs:
            kept(i).wait()
            total = total + known[:, i * wide : (i + 1) * wide].astype(jnp.float32)
        mixed[:, i * wide : (i + 1) * wide] = total.astype(mixed.dtype)
        stored(i).start()
    for i in range(pieces):
        stored(i).wait()


def mix(table, rows, known):
    count = table.shape[0] // 2
    slots, width = rows.shape
    anywhere = pl.BlockSpec(memory_space=pl.ANY)
    vmem = pl.BlockSpec(memory_space=pltpu.VMEM)
    return pl.pallas_call(
        mix_kernel,
        name="mix_slots",
        out_shape=jax.ShapeDtypeStruct((count, width), jnp.bfloat16),
        in_specs=[vmem, anywhere] + [anywhere] * len(known),
        out_specs=anywhere,
        scratch_shapes=[
            pltpu.VMEM((slots, width), jnp.bfloat16),
            pltpu.VMEM((count, width), jnp.bfloat16),
            pltpu.VMEM((count, width), jnp.bfloat16),
            pltpu.SemaphoreType.DMA((PIECES,)),
            pltpu.SemaphoreType.DMA((PIECES,)),
            pltpu.SemaphoreType.DMA((PIECES,)),
        ],
        compiler_params=pltpu.CompilerParams(vmem_limit_bytes=VMEM_BYTES),
        cost_estimate=pl.CostEstimate(
            flops=4 * count * slots * width, transcendentals=0, bytes_accessed=2 * slots * width
        ),
    )(table, rows, *known)


def exchange(rows, devices):
    count, width = rows.shape
    split = rows.reshape(devices, count // devices, width)
    return lax.all_to_all(split, "ep", split_axis=0, concat_axis=0, tiled=True).reshape(
        count, width
    )


def on_device(tokens, expert_ids, affinity, w_gate, w_up, w_down):
    devices = lax.axis_size("ep")
    experts = devices // 2
    slots = 2 * tokens.shape[0] * TOP // experts
    pairs = [(s, s ^ 1) for s in range(devices)]
    gates, ups = [(w, lax.ppermute(w, "ep", pairs)) for w in (w_gate, w_up)]
    turned_ids = expert_ids.T
    table = weights_of_slots(turned_ids, affinity.T, experts, slots, CHUNKS)
    parts = []
    sent = [
        slots_of_tokens(tokens, turned_ids, experts, slots, chunk) for chunk in range(CHUNKS)
    ]
    first, second, late = lax.optimization_barrier((exchange(sent[0], devices), sent[1], w_down))
    downs = (w_down, lax.ppermute(late, "ep", pairs))
    arrived = [first, exchange(second, devices)]
    for rows in arrived:
        parts.append(exchange(expert(rows, gates, ups, downs), devices))
    known = []
    for chunk in range(CHUNKS - 1):
        known = [mix(table[chunk], parts[chunk], known)]
    return mix(table[CHUNKS - 1], parts[CHUNKS - 1], known)


def solution(mesh):
    rows = P(("dp", "ep"), None)
    weights = P("ep", None, None)
    return jax.shard_map(
        on_device,
        mesh=mesh,
        in_specs=(rows, rows, rows, weights, weights, weights),
        out_specs=rows,
        check_vma=False,
    )
```
